128 devices in a mesh: space: 16 (over z_lo, y, core), dir: 4 (over x), band: 2 (over z_hi).
Axes of the slice: x: 4, y: 4, z: 4 (z_hi: 2, z_lo: 2; z = z_hi * 2 + z_lo), core: 2. Of those that a mesh axis runs over, the one named last changes fastest.
Arguments:
- adjoint_start: float32 [64, 32, 96, 1152], P('dir', 'band', 'space'), may hold values from 0.5 to 1.5
- primal_deviations: float32 [64, 32, 96, 1152], P('dir', 'band', 'space'), may hold values from 0.5 to 1.5
- density: float32 [96, 1152], P('space'), may hold values from 0 to 1
- material: int32 [96, 1152], P('space'), may hold values from 0 to 3
- rate_table: float32 [4, 32], P(None, 'band'), may hold values from 0.05 to 2
- group_speed: float32 [32], P('band'), may hold values from 0.3 to 3
- heat_capacity: float32 [32], replicated, may hold values from 0.1 to 4, as said below
- objective_weight: float32 [96, 1152], P('space'), may hold values from -6 to 6
Outputs:
- dual_intensity: float32 [64, 32, 96, 1152], P('dir', 'band', 'space')
- design_gradient: float32 [96, 1152], P('space')
The draws below stay inside these ranges and needn't reach their ends.
Inputs may be any that keep to these rules, and one draw needn't show every extreme that they name: `heat_capacity`: heat capacities of the bands, positive.
All inputs are finite; a program needn't handle non-finite values.
Results may differ from the reference program's by a relative error of at most 0.0003.
Values sent between devices are 32-bit elements; how exact they have to be, the bound alone decides.
A program may use at most 128 MiB of HBM per device.

```python
import math
import jax
import jax.numpy as jnp
from jax import lax

NDIR = 64
NB = 32
NMAT = 4
NY = 192
NZ = 6
ITERS = 2
PLANE = 1152
NX = 96
DIR_DEV = 16


def draw_heat_capacity(key, part):
    index = jnp.arange(NB).astype(jnp.float32)
    factor = jax.random.uniform(key, (NB,), jnp.float32, 0.8, 1.2)
    return 0.3 * jnp.exp(jnp.log(10.0) * index / NB) * factor


def set_ends(drawn, stream_key, least, top_value):
    dims = drawn.shape
    spot = [jax.random.randint(jax.random.fold_in(stream_key, axis), (), 0, dims[axis]) for axis in range(len(dims))]
    drawn = drawn.at[tuple(spot)].set(least)
    longest = dims.index(max(dims))
    spot[longest] = (spot[longest] + 1) % dims[longest]
    return drawn.at[tuple(spot)].set(top_value)


def steps_of(stream_key, dims, cuts, low, high):
    loudness = 1.0
    for dim, shards_of in cuts:
        heights = jax.random.uniform(jax.random.fold_in(jax.random.fold_in(stream_key, 6), dim), (shards_of,), jnp.float32, low / len(cuts), high / len(cuts))
        loudness = loudness * jnp.repeat(jnp.exp(heights), dims[dim] // shards_of).reshape((-1,) + (1,) * (len(dims) - 1 - dim))
    return loudness


def scatter_about(stream_key, dims, scale, most, split=(), kind=jnp.bfloat16):
    result = scale * jax.random.normal(stream_key, dims, jnp.float32)
    if split:
        result = result * steps_of(stream_key, dims, split, -0.22, 0.18)
    return jnp.clip(result, -most, most).astype(kind)


def setup_inputs(seed: int = 0) -> dict:
    keys = jax.random.split(jax.random.key(seed), 9)
    return {
        "adjoint_start": jnp.clip(0.5 + 1.0 * jax.random.uniform(keys[0], (NDIR, NB, NX, PLANE), jnp.float32) ** steps_of(keys[0], (NDIR, NB, NX, PLANE), ((0, 4), (1, 2), (2, 16)), -0.2, 0.2), 0.5, 1.5),
        "primal_deviations": jnp.clip(0.5 + 1.0 * jax.random.uniform(keys[1], (NDIR, NB, NX, PLANE), jnp.float32) ** steps_of(keys[1], (NDIR, NB, NX, PLANE), ((0, 4), (1, 2), (2, 16)), -0.2, 0.2), 0.5, 1.5),
        "density": jnp.clip(1.0 * jax.random.uniform(keys[2], (NX, PLANE), jnp.float32) ** steps_of(keys[2], (NX, PLANE), ((0, 16),), -0.2, 0.2), 0.0, 1.0),
        "material": set_ends(jax.random.randint(keys[3], (NX, PLANE), 0, NMAT), jax.random.fold_in(keys[3], 1), 0, NMAT - 1).astype(jnp.int32),
        "rate_table": jnp.clip(jnp.exp(math.log(2.0) - 3.6888794 * jax.random.uniform(keys[4], (NMAT, NB), jnp.float32) ** steps_of(keys[4], (NMAT, NB), ((1, 2),), -0.2, 0.2)), 0.05, 2.0),
        "group_speed": jnp.clip(jnp.exp(math.log(3.0) - 2.3025851 * jax.random.uniform(keys[5], (NB,), jnp.float32) ** steps_of(keys[5], (NB,), ((0, 2),), -0.2, 0.2)), 0.3, 3.0),
        "heat_capacity": draw_heat_capacity(jax.random.fold_in(keys[8], 71), 0),
        "objective_weight": scatter_about(keys[7], (NX, PLANE), 1.0, 6.0, ((0, 16),), jnp.float32),
    }


def directions():
    index = jnp.arange(NDIR, dtype=jnp.int32)
    half = DIR_DEV // 2
    block = index // DIR_DEV
    slot = index % DIR_DEV
    side = slot // half
    pair = slot % half
    azimuth = jnp.pi * ((block * half + pair).astype(jnp.float32) + 0.5) / (NDIR // 2) - jnp.pi / 2
    along_z = 0.4 * (1.0 - 2.0 * (pair % 2).astype(jnp.float32))
    tilt = jnp.sqrt(1.0 - along_z * along_z)
    along_x = (1.0 - 2.0 * side.astype(jnp.float32)) * tilt * jnp.cos(azimuth)
    along_y = tilt * jnp.sin(azimuth)
    return (along_x, along_y, along_z)

def ahead(field, grid_axis):
    size = field.shape[grid_axis]
    rest = lax.slice_in_dim(field, 1, size, axis=grid_axis)
    return jnp.concatenate([rest, jnp.zeros_like(lax.slice_in_dim(field, 0, 1, axis=grid_axis))], grid_axis)

def behind(field, grid_axis):
    size = field.shape[grid_axis]
    rest = lax.slice_in_dim(field, 0, size - 1, axis=grid_axis)
    return jnp.concatenate([jnp.zeros_like(lax.slice_in_dim(field, 0, 1, axis=grid_axis)), rest], grid_axis)

def plane_move(field, offset):
    last = field.ndim - 1
    size = field.shape[last]
    if offset > 0:
        rest = lax.slice_in_dim(field, offset, size, axis=last)
        pad_block = jnp.zeros_like(lax.slice_in_dim(field, 0, offset, axis=last))
        return jnp.concatenate([rest, pad_block], last)
    rest = lax.slice_in_dim(field, 0, size + offset, axis=last)
    pad_block = jnp.zeros_like(lax.slice_in_dim(field, 0, -offset, axis=last))
    return jnp.concatenate([pad_block, rest], last)

def reference(adjoint_start, primal_deviations, density, material, rate_table, group_speed, heat_capacity, objective_weight):
    along_x, along_y, along_z = directions()
    position = jnp.arange(NZ * NY, dtype=jnp.int32) % NY
    keep_ahead = (position < NY - 1).astype(jnp.float32)
    keep_behind = (position > 0).astype(jnp.float32)
    indicator = (material[None] == jnp.arange(NMAT, dtype=jnp.int32)[:, None, None]).astype(jnp.float32)
    base = jnp.einsum('mb,mxp->bxp', rate_table, indicator, precision=lax.Precision.HIGHEST)
    relaxation_frequency = base * (0.2 + 0.8 * density)[None]
    relaxation_slope = 0.8 * base
    weights = heat_capacity / (NDIR * jnp.sum(heat_capacity))
    column = weights[:, None, None]
    speed = group_speed[:, None, None]

    def thermal_share(spatial_excess):
        return lax.optimization_barrier(jnp.sum(column * spatial_excess, axis=0))

    def relaxation_share(field):
        return lax.optimization_barrier(jnp.sum(relaxation_frequency * field, axis=0))
    crystal_kelvin = lax.optimization_barrier(jnp.sum(lax.map(thermal_share, primal_deviations), axis=0))
    exchange_link = lax.optimization_barrier(jnp.sum(lax.map(relaxation_share, adjoint_start), axis=0))
    cell_source = NDIR * NB * objective_weight
    dual_intensity = adjoint_start
    gradient = jnp.zeros_like(density)
    for step in range(ITERS):
        source = column * (exchange_link + cell_source)[None]

        def one_direction(item):
            comp_x, comp_y, comp_z, field, spatial_excess = item
            speed_x = speed * jnp.abs(comp_x)
            speed_y = speed * jnp.abs(comp_y)
            speed_z = speed * jnp.abs(comp_z)
            near = speed_x * jnp.where(comp_x > 0, ahead(field, 1), behind(field, 1))
            near = near + speed_y * jnp.where(comp_y > 0, plane_move(field, 1) * keep_ahead, plane_move(field, -1) * keep_behind)
            near = near + speed_z * jnp.where(comp_z > 0, plane_move(field, NY), plane_move(field, -NY))
            refreshed_excess = (source + near) / (speed_x + speed_y + speed_z + relaxation_frequency)
            return (refreshed_excess, lax.optimization_barrier(jnp.sum(relaxation_frequency * refreshed_excess, axis=0)), lax.optimization_barrier(jnp.sum(relaxation_slope * refreshed_excess * (spatial_excess - crystal_kelvin[None]), axis=0)))
        dual_intensity, rate_parts, term_parts = lax.map(one_direction, (along_x, along_y, along_z, dual_intensity, primal_deviations))
        exchange_link = lax.optimization_barrier(jnp.sum(rate_parts, axis=0))
        gradient = gradient + lax.optimization_barrier(jnp.sum(term_parts, axis=0))
    return (dual_intensity, gradient * (-0.125 / ITERS))
```

```python
import jax
import jax.numpy as jnp
import numpy as np
from jax import lax
from jax.experimental import pallas as pl
from jax.experimental.pallas import tpu as pltpu
from jax.sharding import PartitionSpec as P

NDIR = 64
NB = 32
NY = 192
ITERS = 2
LANES = 128
SUB = 8
MESH = pl.DeviceIdType.MESH


def direction_constants(half, blocks):
    index = np.arange(blocks * half, dtype=np.float32)
    azimuth = np.float32(np.pi) * (index + np.float32(0.5)) / np.float32(NDIR // 2)
    azimuth = azimuth - np.float32(np.pi / 2)
    pair = np.arange(blocks * half) % half
    along_z = np.float32(0.4) * (1 - 2 * (pair % 2)).astype(np.float32)
    tilt = np.sqrt(np.float32(1.0) - along_z * along_z)
    along_x = np.abs(tilt * np.cos(azimuth))
    along_y = np.abs(tilt * np.sin(azimuth))
    return (
        along_x.reshape(blocks, half),
        along_y.reshape(blocks, half),
        np.abs(along_z).reshape(blocks, half),
    )


def by_block(block, values):
    chosen = jnp.float32(values[-1])
    for index in range(len(values) - 2, -1, -1):
        chosen = jnp.where(block == index, jnp.float32(values[index]), chosen)
    return chosen


def make_kernel(ndir, nbands, nx, plane, n_space, n_dir, n_band):
    half = ndir // 2
    tiles = plane // LANES
    subs = nbands // SUB
    last = nx - 1
    const_x, const_y, const_z = direction_constants(half, n_dir)

    def kernel(
        adj, pri, den, mat, rt, gs, hc, ow,
        out, grad,
        A, PV, D, R, RATE, BASE, WS, CF, SUMA, SUMP, TB, ACCB, ACCG,
        denv, matv, rtv, gsv, hcv, owv, gradv,
        XB, ZB,
        load_sem, small_sem, h_send, h_recv, x_send, x_recv, z_send, z_recv, out_sem, grad_sem,
    ):
        space = lax.axis_index("space")
        block = lax.axis_index("dir")
        band = lax.axis_index("band")
        other_band = 1 - band

        barrier = pltpu.get_barrier_semaphore()
        for k in range(1, n_dir):
            peer = lax.rem(block + k, n_dir)
            pl.semaphore_signal(barrier, inc=1, device_id={"dir": peer}, device_id_type=MESH)
        pl.semaphore_signal(barrier, inc=1, device_id={"band": other_band}, device_id_type=MESH)

        @pl.when(space > 0)
        def _():
            pl.semaphore_signal(barrier, inc=1, device_id={"space": space - 1}, device_id_type=MESH)

        @pl.when(space < n_space - 1)
        def _():
            pl.semaphore_signal(barrier, inc=1, device_id={"space": space + 1}, device_id_type=MESH)

        smalls = [
            pltpu.make_async_copy(src, dst, small_sem.at[i])
            for i, (src, dst) in enumerate(
                ((den, denv), (mat, matv), (rt, rtv), (gs, gsv), (hc, hcv), (ow, owv))
            )
        ]
        group = 4
        loads_a = []
        loads_p = []
        for g in range(ndir // group):
            first = g * group
            shift = 0 if first < half else 1
            loads_a.append(
                pltpu.make_async_copy(
                    adj.at[pl.ds(first, group)],
                    A.at[pl.ds(first, group), pl.ds(shift, nx)],
                    load_sem.at[0, g],
                )
            )
            loads_p.append(
                pltpu.make_async_copy(
                    pri.at[pl.ds(first, group)], PV.at[pl.ds(first, group)], load_sem.at[1, g]
                )
            )
        for copy in smalls:
            copy.start()
        for copy in loads_a:
            copy.start()
        for copy in loads_p:
            copy.start()

        at_end = jnp.logical_or(space == 0, space == n_space - 1)

        @pl.when(at_end)
        def _():
            pl.semaphore_wait(barrier, n_dir + 1)

        @pl.when(jnp.logical_not(at_end))
        def _():
            pl.semaphore_wait(barrier, n_dir + 2)

        def halo(step, down, source=None):
            buffer = D if step else A
            if down:
                src = adj.at[pl.ds(0, half), 0] if step == 0 else D.at[pl.ds(0, half), 0]
                return pltpu.make_async_remote_copy(
                    src_ref=src,
                    dst_ref=buffer.at[pl.ds(0, half), nx],
                    send_sem=h_send.at[step, 0],
                    recv_sem=h_recv.at[step, 0],
                    device_id={"space": space - 1},
                    device_id_type=MESH,
                )
            src = adj.at[pl.ds(half, half), last] if step == 0 else D.at[pl.ds(half, half), nx]
            return pltpu.make_async_remote_copy(
                src_ref=src,
                dst_ref=buffer.at[pl.ds(half, half), 0],
                send_sem=h_send.at[step, 1],
                recv_sem=h_recv.at[step, 1],
                device_id={"space": space + 1},
                device_id_type=MESH,
            )

        def halo_start(step):
            @pl.when(space > 0)
            def _():
                halo(step, True).start()

            @pl.when(space < n_space - 1)
            def _():
                halo(step, False).start()

        def halo_wait_recv(step):
            @pl.when(space < n_space - 1)
            def _():
                halo(step, True).wait_recv()

            @pl.when(space > 0)
            def _():
                halo(step, False).wait_recv()

        def halo_wait_send(step):
            @pl.when(space > 0)
            def _():
                halo(step, True).wait_send()

            @pl.when(space < n_space - 1)
            def _():
                halo(step, False).wait_send()

        halo_start(0)

        @pl.when(space == n_space - 1)
        def _():
            def clear(d, carry):
                A[d, nx] = jnp.zeros((nbands, plane), jnp.float32)
                D[d, nx] = jnp.zeros((nbands, plane), jnp.float32)
                return carry

            lax.fori_loop(0, half, clear, 0)

        @pl.when(space == 0)
        def _():
            def clear(d, carry):
                A[half + d, 0] = jnp.zeros((nbands, plane), jnp.float32)
                D[half + d, 0] = jnp.zeros((nbands, plane), jnp.float32)
                return carry

            lax.fori_loop(0, half, clear, 0)

        for copy in smalls:
            copy.wait()
        row_index = lax.broadcasted_iota(jnp.int32, (nbands, nbands), 0)
        lane_index = lax.broadcasted_iota(jnp.int32, (nbands, nbands), 1)

        def column(row):
            spread = jnp.where(row_index == lane_index, row, 0.0)
            return jnp.broadcast_to(jnp.sum(spread, axis=1, keepdims=True), (nbands, LANES))

        rates = [column(rtv[m : m + 1, :]) for m in range(rt.shape[0])]
        speed = column(gsv[...])
        heat = hcv[...]
        total_heat = jnp.sum(heat, axis=1, keepdims=True)
        wide_row = lax.broadcasted_iota(jnp.int32, (nbands, NB), 0) + band * nbands
        wide_lane = lax.broadcasted_iota(jnp.int32, (nbands, NB), 1)
        local_heat = jnp.sum(jnp.where(wide_row == wide_lane, heat, 0.0), axis=1, keepdims=True)
        weight = jnp.broadcast_to(local_heat / (NDIR * total_heat), (nbands, LANES))
        lane = lax.broadcasted_iota(jnp.int32, (nbands, LANES), 1)
        ahead = block >= n_dir // 2
        middle = jnp.where(ahead, 63, 64)
        edge = jnp.where(ahead, LANES - 1, 0)
        for pair in range(half):
            sx = speed * by_block(block, const_x[:, pair])
            sy = speed * by_block(block, const_y[:, pair])
            sz = speed * jnp.float32(const_z[0, pair])
            CF[pair, 0] = sx
            CF[pair, 1] = sy
            CF[pair, 2] = jnp.where(lane == middle, 0.0, sy)
            CF[pair, 3] = jnp.where(lane == edge, 0.0, sy)
            CF[pair, 4] = sz
            CF[pair, 5] = sx + sy + sz

        for x in range(nx):
            for j in range(tiles):
                cut = slice(j * LANES, (j + 1) * LANES)
                kind = jnp.broadcast_to(matv[x : x + 1, cut], (nbands, LANES))
                base = rates[-1]
                for m in range(rt.shape[0] - 2, -1, -1):
                    base = jnp.where(kind == m, rates[m], base)
                BASE[x, :, cut] = base
                RATE[x, :, cut] = base * (0.2 + 0.8 * denv[x : x + 1, cut])

        def sum_group(source, target, g, shift):
            def body(x, carry):
                total = source[g * group, x + shift]
                for d in range(1, group):
                    total = total + source[g * group + d, x + shift]
                if g:
                    total = total + target[x]
                target[x] = total
                return carry

            lax.fori_loop(0, nx, body, 0)

        def x_copy(n, k):
            return pltpu.make_async_remote_copy(
                src_ref=XB.at[n, block],
                dst_ref=XB.at[n, block],
                send_sem=x_send.at[n, k - 1],
                recv_sem=x_recv.at[n, k - 1],
                device_id={"dir": lax.rem(block + k, n_dir)},
                device_id_type=MESH,
            )

        def z_copy(n):
            return pltpu.make_async_remote_copy(
                src_ref=ZB.at[n, band],
                dst_ref=ZB.at[n, band],
                send_sem=z_send.at[n],
                recv_sem=z_recv.at[n],
                device_id={"band": other_band},
                device_id_type=MESH,
            )

        def exchange_start(n):
            for k in range(1, n_dir):
                x_copy(n, k).start()

        def exchange_middle(n):
            for k in range(1, n_dir):
                x_copy(n, k).wait_recv()
            total = XB[n, 0]
            for k in range(1, n_dir):
                total = total + XB[n, k]
            ZB[n, band] = total
            z_copy(n).start()

        def exchange_end(n):
            z_copy(n).wait_recv()
            return ZB[n, 0] + ZB[n, 1]

        def exchange_drain(n):
            for k in range(1, n_dir):
                x_copy(n, k).wait_send()
            z_copy(n).wait_send()

        wide_weight = jnp.concatenate([weight] * tiles, axis=1)

        for g in range(ndir // group):
            loads_a[g].wait()
            sum_group(A, SUMA, g, 0 if g * group < half else 1)
        for x in range(nx):
            XB[0, block, x : x + 1, :] = jnp.sum(RATE[x] * SUMA[x], axis=0, keepdims=True)
        exchange_start(0)
        for g in range(ndir // group):
            loads_p[g].wait()
            sum_group(PV, SUMP, g, 0)
        for x in range(nx):
            XB[1, block, x : x + 1, :] = jnp.sum(wide_weight * SUMP[x], axis=0, keepdims=True)
        exchange_start(1)

        def set_source(coupling):
            source = coupling + NDIR * NB * owv[...]
            for x in range(nx):
                WS[x] = wide_weight * source[x : x + 1]

        for x in range(nx):
            ACCB[x] = jnp.zeros((SUB, plane), jnp.float32)
            ACCG[x] = jnp.zeros((SUB, plane), jnp.float32)

        exchange_middle(0)
        exchange_middle(1)
        set_source(exchange_end(0))
        temperature = exchange_end(1)
        for x in range(nx):
            TB[x] = jnp.broadcast_to(temperature[x : x + 1], (SUB, plane))

        low_lanes = lax.broadcasted_iota(jnp.int32, (SUB, LANES), 1) < LANES // 2
        edge_first = lax.broadcasted_iota(jnp.int32, (SUB, LANES), 1) == 0
        edge_last = lax.broadcasted_iota(jnp.int32, (SUB, LANES), 1) == LANES - 1

        def slab(step, forward_y, side, pair, up_z, x, acc_b, acc_g):
            source, target = (A, D) if step == 0 else (D, A)
            d = pair + side * half
            own = x + side
            beside = x + 1 - side
            for s in range(subs):
                rows = pl.ds(s * SUB, SUB)
                field = source[d, own, rows, :]
                near_x = source[d, beside, rows, :]
                cx = CF[pair, 0, rows, :]
                cy = [CF[pair, 1 + i, rows, :] for i in range(3)]
                cz = CF[pair, 4, rows, :]
                csum = CF[pair, 5, rows, :]
                rate = RATE[x, rows, :]
                base = BASE[x, rows, :]
                ws = WS[x, rows, :]
                excess = PV[d, x, rows, :]
                warm = TB[x]
                if step:
                    recip = R[d, x, rows, :]
                cut = [slice(j * LANES, (j + 1) * LANES) for j in range(tiles)]
                parts = [field[:, c] for c in cut]
                turn = [pltpu.roll(v, LANES - 1 if forward_y else 1, 1) for v in parts]
                halfway = [pltpu.roll(v, LANES // 2, 1) for v in parts]
                results = []
                recips = []
                for j in range(tiles):
                    if forward_y:
                        coef = cy[(0, 1, 2)[j % 3]]
                        moved = turn[j]
                        if j % 3 != 2:
                            moved = jnp.where(edge_last, turn[j + 1], moved)
                    else:
                        coef = cy[(2, 1, 0)[j % 3]]
                        moved = turn[j]
                        if j % 3 != 0:
                            moved = jnp.where(edge_first, turn[j - 1], moved)
                    value = ws[:, cut[j]] + cx * near_x[:, cut[j]]
                    value = value + coef * moved
                    if up_z:
                        if j + 2 < tiles:
                            value = value + cz * jnp.where(low_lanes, halfway[j + 1], halfway[j + 2])
                        elif j + 1 < tiles:
                            value = value + cz * jnp.where(low_lanes, halfway[j + 1], 0.0)
                    else:
                        if j >= 2:
                            value = value + cz * jnp.where(low_lanes, halfway[j - 2], halfway[j - 1])
                        elif j >= 1:
                            value = value + cz * jnp.where(low_lanes, 0.0, halfway[j - 1])
                    if step == 0:
                        diagonal = csum + rate[:, cut[j]]
                        guess = pl.reciprocal(diagonal, approx=True)
                        inverse = guess * (2.0 - diagonal * guess)
                        recips.append(inverse)
                    else:
                        inverse = recip[:, cut[j]]
                    value = value * inverse
                    results.append(value)
                    share = base[:, cut[j]] * value
                    if step == 0:
                        acc_b[j] = acc_b[j] + share
                    acc_g[j] = acc_g[j] + share * (excess[:, cut[j]] - warm[:, cut[j]])
                target[d, own, rows, :] = jnp.concatenate(results, axis=1)
                if step == 0:
                    R[d, x, rows, :] = jnp.concatenate(recips, axis=1)
            return acc_b, acc_g

        def sweep(step, forward_y):
            def layer(i, carry):
                @pl.when(i == last)
                def _():
                    halo_wait_recv(step)

                for side in range(2):
                    x = i if side == 0 else last - i

                    def pairs(k, accs):
                        acc_b, acc_g = list(accs[0]), list(accs[1])
                        for up in range(2):
                            acc_b, acc_g = slab(
                                step, forward_y, side, 2 * k + up, up == 0, x, acc_b, acc_g
                            )
                        return (tuple(acc_b), tuple(acc_g))

                    zero = tuple(jnp.zeros((SUB, LANES), jnp.float32) for _ in range(tiles))
                    acc_b, acc_g = lax.fori_loop(0, half // 2, pairs, (zero, zero))
                    if step == 0:
                        ACCB[x] = ACCB[x] + jnp.concatenate(acc_b, axis=1)
                    ACCG[x] = ACCG[x] + jnp.concatenate(acc_g, axis=1)
                    if step:
                        out_copy(side, x).start()
                if step == 0:

                    @pl.when(i == 0)
                    def _():
                        halo_start(1)

                return carry

            lax.fori_loop(0, nx, layer, 0)

        def out_copy(side, x):
            return pltpu.make_async_copy(
                A.at[pl.ds(side * half, half), x + side],
                out.at[pl.ds(side * half, half), x],
                out_sem.at[side, x],
            )

        def both(step):
            @pl.when(ahead)
            def _():
                sweep(step, True)

            @pl.when(jnp.logical_not(ahead))
            def _():
                sweep(step, False)

        both(0)
        for x in range(nx):
            summed = jnp.sum(ACCB[x], axis=0, keepdims=True)
            XB[2, block, x : x + 1, :] = summed * (0.2 + 0.8 * denv[x : x + 1, :])
        exchange_start(2)
        exchange_middle(2)
        set_source(exchange_end(2))
        halo_wait_send(0)
        both(1)
        for x in range(nx):
            XB[3, block, x : x + 1, :] = 0.8 * jnp.sum(ACCG[x], axis=0, keepdims=True)
        exchange_start(3)
        exchange_middle(3)
        gradv[...] = exchange_end(3) * (-0.125 / ITERS)
        final = pltpu.make_async_copy(gradv, grad, grad_sem)
        final.start()
        for n in range(4):
            exchange_drain(n)
        halo_wait_send(1)
        for side in range(2):
            for x in range(nx):
                out_copy(side, x).wait()
        final.wait()

    return kernel


def solution(mesh):
    n_space, n_dir, n_band = mesh.shape["space"], mesh.shape["dir"], mesh.shape["band"]
    placed = (
        P("dir", "band", "space", None),
        P("dir", "band", "space", None),
        P("space", None),
        P("space", None),
        P(None, "band"),
        P("band"),
        P(),
        P("space", None),
    )

    def on_device(adj, pri, den, mat, rt, gs, hc, ow):
        ndir, nbands, nx, plane = adj.shape
        half = ndir // 2
        f32 = jnp.float32
        vmem = lambda *shape: pltpu.VMEM(shape, f32)
        dma = pltpu.SemaphoreType.DMA
        call = pl.pallas_call(
            make_kernel(ndir, nbands, nx, plane, n_space, n_dir, n_band),
            out_shape=(
                jax.ShapeDtypeStruct((ndir, nx, nbands, plane), f32),
                jax.ShapeDtypeStruct((nx, plane), f32),
            ),
            in_specs=[pl.BlockSpec(memory_space=pl.ANY)] * 8,
            out_specs=(pl.BlockSpec(memory_space=pl.ANY),) * 2,
            scratch_shapes=[
                vmem(ndir, nx + 1, nbands, plane),
                vmem(ndir, nx, nbands, plane),
                vmem(ndir, nx + 1, nbands, plane),
                vmem(ndir, nx, nbands, plane),
                vmem(nx, nbands, plane),
                vmem(nx, nbands, plane),
                vmem(nx, nbands, plane),
                vmem(half, 6, nbands, LANES),
                vmem(nx, nbands, plane),
                vmem(nx, nbands, plane),
                vmem(nx, SUB, plane),
                vmem(nx, SUB, plane),
                vmem(nx, SUB, plane),
                vmem(nx, plane),
                pltpu.VMEM((nx, plane), jnp.int32),
                vmem(*rt.shape),
                vmem(1, nbands),
                vmem(1, NB),
                vmem(nx, plane),
                vmem(nx, plane),
                vmem(4, n_dir, nx, plane),
                vmem(4, n_band, nx, plane),
                dma((2, 4)),
                dma((6,)),
                dma((2, 2)),
                dma((2, 2)),
                dma((4, n_dir - 1)),
                dma((4, n_dir - 1)),
                dma((4,)),
                dma((4,)),
                dma((2, nx)),
                dma,
            ],
            compiler_params=pltpu.CompilerParams(
                collective_id=0, has_side_effects=True, vmem_limit_bytes=60 * 1024 * 1024
            ),
        )
        turn = lambda v: jnp.transpose(v, (0, 2, 1, 3))
        dual, grad = call(
            turn(adj), turn(pri), den, mat, rt, gs.reshape(1, nbands), hc.reshape(1, NB), ow
        )
        return turn(dual), grad

    return jax.shard_map(
        on_device,
        mesh=mesh,
        in_specs=placed,
        out_specs=(P("dir", "band", "space", None), P("space", None)),
        check_vma=False,
    )
```

```python
import jax
import jax.numpy as jnp
import numpy as np
from jax import lax
from jax.experimental import pallas as pl
from jax.experimental.pallas import tpu as pltpu
from jax.sharding import PartitionSpec as P

NDIR = 64
NB = 32
NY = 192
ITERS = 2
LANES = 128
SUB = 8
MIDDLE0 = 3
MIDDLE1 = 2
MESH = pl.DeviceIdType.MESH


def direction_constants(half, blocks):
    index = np.arange(blocks * half, dtype=np.float32)
    azimuth = np.float32(np.pi) * (index + np.float32(0.5)) / np.float32(NDIR // 2)
    azimuth = azimuth - np.float32(np.pi / 2)
    pair = np.arange(blocks * half) % half
    along_z = np.float32(0.4) * (1 - 2 * (pair % 2)).astype(np.float32)
    tilt = np.sqrt(np.float32(1.0) - along_z * along_z)
    along_x = np.abs(tilt * np.cos(azimuth))
    along_y = np.abs(tilt * np.sin(azimuth))
    return (
        along_x.reshape(blocks, half),
        along_y.reshape(blocks, half),
        np.abs(along_z).reshape(blocks, half),
    )


def by_block(block, values):
    chosen = jnp.float32(values[-1])
    for index in range(len(values) - 2, -1, -1):
        chosen = jnp.where(block == index, jnp.float32(values[index]), chosen)
    return chosen


def make_kernel(ndir, nbands, nx, plane, n_space, n_dir, n_band):
    half = ndir // 2
    tiles = plane // LANES
    subs = nbands // SUB
    last = nx - 1
    const_x, const_y, const_z = direction_constants(half, n_dir)

    def kernel(
        adj, pri, den, mat, rt, gs, hc, ow,
        out, grad,
        A, PV, D, R, RATE, BASE, WS, CF, SUMA, SUMP, SUMR, SUMG, TB, SV, SH, HS, HR,
        denv, matv, rtv, gsv, hcv, owv,
        XB, ZB,
        load_sem, small_sem, h_send, h_recv, r_send, r_recv, x_send, x_recv, z_send, z_recv,
    ):
        space = lax.axis_index("space")
        block = lax.axis_index("dir")
        band = lax.axis_index("band")
        other_band = 1 - band
        has_low = space > 0
        has_high = space < n_space - 1

        barrier = pltpu.get_barrier_semaphore()
        for k in range(1, n_dir):
            peer = lax.rem(block + k, n_dir)
            pl.semaphore_signal(barrier, inc=1, device_id={"dir": peer}, device_id_type=MESH)
        pl.semaphore_signal(barrier, inc=1, device_id={"band": other_band}, device_id_type=MESH)

        @pl.when(has_low)
        def _():
            pl.semaphore_signal(barrier, inc=1, device_id={"space": space - 1}, device_id_type=MESH)

        @pl.when(has_high)
        def _():
            pl.semaphore_signal(barrier, inc=1, device_id={"space": space + 1}, device_id_type=MESH)

        smalls = [
            pltpu.make_async_copy(src, dst, small_sem.at[i])
            for i, (src, dst) in enumerate(
                ((den, denv), (mat, matv), (rt, rtv), (gs, gsv), (hc, hcv), (ow, owv))
            )
        ]
        group = 4
        loads_a = []
        loads_p = []
        for g in range(ndir // group):
            first = g * group
            shift = 0 if first < half else 1
            loads_a.append(
                pltpu.make_async_copy(
                    adj.at[pl.ds(first, group)],
                    A.at[pl.ds(first, group), pl.ds(shift, nx)],
                    load_sem.at[0, g],
                )
            )
            loads_p.append(
                pltpu.make_async_copy(
                    pri.at[pl.ds(first, group)], PV.at[pl.ds(first, group)], load_sem.at[1, g]
                )
            )
        for copy in smalls:
            copy.start()
        for copy in loads_a:
            copy.start()
        for copy in loads_p:
            copy.start()

        with jax.named_scope("barrier"):
            at_end = jnp.logical_or(space == 0, space == n_space - 1)

            @pl.when(at_end)
            def _():
                pl.semaphore_wait(barrier, n_dir + 1)

            @pl.when(jnp.logical_not(at_end))
            def _():
                pl.semaphore_wait(barrier, n_dir + 2)

        def beside(src, dst, down, send_sem, recv_sem):
            return pltpu.make_async_remote_copy(
                src_ref=src,
                dst_ref=dst,
                send_sem=send_sem,
                recv_sem=recv_sem,
                device_id={"space": space - 1 if down else space + 1},
                device_id_type=MESH,
            )

        def halo(step, down):
            way = 0 if down else 1
            rows = pl.ds(0 if down else half, half)
            buffer = D if step else A
            if step:
                src = D.at[rows, 0 if down else nx]
            else:
                src = adj.at[rows, 0 if down else last]
            dst = buffer.at[rows, nx if down else 0]
            return beside(src, dst, down, h_send.at[step, way], h_recv.at[step, way])

        def rows_copy(step, down):
            way = 0 if down else 1
            if step == 0:
                src, dst = HS.at[way], HR.at[way]
            else:
                src, dst = SV.at[0 if down else last], SH.at[way]
            return beside(src, dst, down, r_send.at[step, way], r_recv.at[step, way])

        def both_ways(make, act, receive=False):
            @pl.when(has_high if receive else has_low)
            def _():
                act(make(True))

            @pl.when(has_low if receive else has_high)
            def _():
                act(make(False))

        def start(make):
            both_ways(make, lambda copy: copy.start())

        def arrive(make):
            both_ways(make, lambda copy: copy.wait_recv(), receive=True)

        def drain(make):
            both_ways(make, lambda copy: copy.wait_send())

        with jax.named_scope("halo0"):
            start(lambda down: halo(0, down))

        @pl.when(jnp.logical_not(has_high))
        def _():
            def clear(d, carry):
                for buffer in (A, D, R):
                    buffer[d, nx] = jnp.zeros((nbands, plane), jnp.float32)
                return carry

            lax.fori_loop(0, half, clear, 0)

        @pl.when(jnp.logical_not(has_low))
        def _():
            def clear(d, carry):
                for buffer in (A, D, R):
                    buffer[half + d, 0] = jnp.zeros((nbands, plane), jnp.float32)
                return carry

            lax.fori_loop(0, half, clear, 0)

        with jax.named_scope("smallwait"):
            for copy in smalls:
                copy.wait()
        with jax.named_scope("tables"):
            for way, x in ((0, 0), (1, last)):
                HS[way, 0] = denv[x : x + 1, :]
                HS[way, 1] = matv[x : x + 1, :].astype(jnp.float32)
            start(lambda down: rows_copy(0, down))
            row_index = lax.broadcasted_iota(jnp.int32, (nbands, nbands), 0)
            lane_index = lax.broadcasted_iota(jnp.int32, (nbands, nbands), 1)

            def column(row):
                spread = jnp.where(row_index == lane_index, row, 0.0)
                return jnp.broadcast_to(jnp.sum(spread, axis=1, keepdims=True), (nbands, LANES))

            rates = [column(rtv[m : m + 1, :]) for m in range(rt.shape[0])]
            speed = column(gsv[...])
            heat = hcv[...]
            total_heat = jnp.sum(heat, axis=1, keepdims=True)
            wide_row = lax.broadcasted_iota(jnp.int32, (nbands, NB), 0) + band * nbands
            wide_lane = lax.broadcasted_iota(jnp.int32, (nbands, NB), 1)
            local_heat = jnp.sum(jnp.where(wide_row == wide_lane, heat, 0.0), axis=1, keepdims=True)
            weight = jnp.broadcast_to(local_heat / (NDIR * total_heat), (nbands, LANES))
            wide_weight = jnp.concatenate([weight] * tiles, axis=1)
            lane = lax.broadcasted_iota(jnp.int32, (nbands, LANES), 1)
            ahead = block >= n_dir // 2
            middle = jnp.where(ahead, 63, 64)
            edge = jnp.where(ahead, LANES - 1, 0)
            for pair in range(half):
                sx = speed * by_block(block, const_x[:, pair])
                sy = speed * by_block(block, const_y[:, pair])
                sz = speed * jnp.float32(const_z[0, pair])
                CF[pair, 0] = sx
                CF[pair, 1] = sy
                CF[pair, 2] = jnp.where(lane == middle, 0.0, sy)
                CF[pair, 3] = jnp.where(lane == edge, 0.0, sy)
                CF[pair, 4] = sz
                CF[pair, 5] = sx + sy + sz

            def base_of(kind_row, j):
                kind = jnp.broadcast_to(kind_row, (nbands, LANES))
                base = rates[-1]
                for m in range(rt.shape[0] - 2, -1, -1):
                    base = jnp.where(kind == m, rates[m], base)
                return base

            cuts = [slice(j * LANES, (j + 1) * LANES) for j in range(tiles)]
            for x in range(nx):
                for j in range(tiles):
                    base = base_of(matv[x : x + 1, cuts[j]], j)
                    BASE[x, :, cuts[j]] = base
                    RATE[x, :, cuts[j]] = base * (0.2 + 0.8 * denv[x : x + 1, cuts[j]])

        def sum_group(source, target, g, shift):
            def body(x, carry):
                total = source[g * group, x + shift]
                for d in range(1, group):
                    total = total + source[g * group + d, x + shift]
                if g:
                    total = total + target[x]
                target[x] = total
                return carry

            lax.fori_loop(0, nx, body, 0)

        def x_copy(n, k):
            ref = XB.at[n, block] if n < 2 else XB.at[n, block, 0]
            return pltpu.make_async_remote_copy(
                src_ref=ref,
                dst_ref=ref,
                send_sem=x_send.at[n, k - 1],
                recv_sem=x_recv.at[n, k - 1],
                device_id={"dir": lax.rem(block + k, n_dir)},
                device_id_type=MESH,
            )

        def z_copy(n):
            ref = ZB.at[n, band] if n < 2 else ZB.at[n, band, 0]
            return pltpu.make_async_remote_copy(
                src_ref=ref,
                dst_ref=ref,
                send_sem=z_send.at[n],
                recv_sem=z_recv.at[n],
                device_id={"band": other_band},
                device_id_type=MESH,
            )

        def exchange_start(n):
            for k in range(1, n_dir):
                x_copy(n, k).start()

        def exchange_middle(n):
            for k in range(1, n_dir):
                x_copy(n, k).wait_recv()
            for part in range(2 if n < 2 else 1):
                total = XB[n, 0, part]
                for k in range(1, n_dir):
                    total = total + XB[n, k, part]
                ZB[n, band, part] = total
            z_copy(n).start()

        def exchange_end(n):
            z_copy(n).wait_recv()
            return [ZB[n, 0, part] + ZB[n, 1, part] for part in range(2 if n < 2 else 1)]

        def exchange_drain(n):
            for k in range(1, n_dir):
                x_copy(n, k).wait_send()
            z_copy(n).wait_send()

        def fold(n, part, x, value):
            XB[n, block, part, x : x + 1, :] = jnp.sum(value, axis=0, keepdims=True)

        with jax.named_scope("sum_a"):
            for g in range(ndir // group):
                loads_a[g].wait()
                sum_group(A, SUMA, g, 0 if g * group < half else 1)
            for x in range(nx):
                fold(0, 0, x, RATE[x] * SUMA[x])
        with jax.named_scope("sum_p"):
            for g in range(ndir // group):
                loads_p[g].wait()
                sum_group(PV, SUMP, g, 0)
            for x in range(nx):
                fold(0, 1, x, wide_weight * SUMP[x])
            exchange_start(0)

        for x in range(nx):
            for buffer in (SUMA, SUMR, SUMP, SUMG):
                buffer[x] = jnp.zeros((nbands, plane), jnp.float32)

        lane8 = lax.broadcasted_iota(jnp.int32, (SUB, LANES), 1)
        low_lanes = lane8 < LANES // 2
        edge_first = lane8 == 0
        edge_last = lane8 == LANES - 1

        def reciprocal(diagonal):
            guess = pl.reciprocal(diagonal, approx=True)
            return guess * (2.0 - diagonal * guess)

        def stream(forward_y, up_z, pair, rows, field, near_x):
            cx = CF[pair, 0, rows, :]
            cy = [CF[pair, 1 + i, rows, :] for i in range(3)]
            cz = CF[pair, 4, rows, :]
            turn = [pltpu.roll(v, LANES - 1 if forward_y else 1, 1) for v in field]
            halfway = [pltpu.roll(v, LANES // 2, 1) for v in field]
            values = []
            for j in range(tiles):
                moved = turn[j]
                if forward_y:
                    coef = cy[(0, 1, 2)[j % 3]]
                    if j % 3 != 2:
                        moved = jnp.where(edge_last, turn[j + 1], moved)
                else:
                    coef = cy[(2, 1, 0)[j % 3]]
                    if j % 3 != 0:
                        moved = jnp.where(edge_first, turn[j - 1], moved)
                value = cx * near_x[j] + coef * moved
                if up_z:
                    if j + 2 < tiles:
                        value = value + cz * jnp.where(low_lanes, halfway[j + 1], halfway[j + 2])
                    elif j + 1 < tiles:
                        value = value + cz * jnp.where(low_lanes, halfway[j + 1], 0.0)
                else:
                    if j >= 2:
                        value = value + cz * jnp.where(low_lanes, halfway[j - 2], halfway[j - 1])
                    elif j >= 1:
                        value = value + cz * jnp.where(low_lanes, 0.0, halfway[j - 1])
                values.append(value)
            return values

        def split(ref_rows):
            return [ref_rows[:, c] for c in cuts]

        def join(parts):
            return jnp.concatenate(parts, axis=1)

        def slab_a(forward_y, side, x):
            for s in range(subs):
                rows = pl.ds(s * SUB, SUB)
                rate = split(RATE[x, rows, :])
                total_a, total_r = None, None
                for pair in range(half):
                    d = pair + side * half
                    own, other = x + side, x + 1 - side
                    csum = CF[pair, 5, rows, :]
                    near = stream(
                        forward_y, pair % 2 == 0, pair, rows, split(A[d, own, rows, :]), split(A[d, other, rows, :])
                    )
                    inverse = [reciprocal(csum + rate[j]) for j in range(tiles)]
                    value = join([near[j] * inverse[j] for j in range(tiles)])
                    inverse = join(inverse)
                    D[d, own, rows, :] = value
                    R[d, own, rows, :] = inverse
                    total_a = value if pair == 0 else total_a + value
                    total_r = inverse if pair == 0 else total_r + inverse
                SUMA[x, rows, :] = SUMA[x, rows, :] + total_a
                SUMR[x, rows, :] = SUMR[x, rows, :] + total_r

        def slab_b(forward_y, side, x):
            warm = split(TB[x])
            for s in range(subs):
                rows = pl.ds(s * SUB, SUB)
                source = split(WS[x + 2 - 2 * side, rows, :])
                own_source = split(WS[x + 1, rows, :])
                total_g, total_e = None, None
                for pair in range(half):
                    d = pair + side * half
                    own, other = x + side, x + 1 - side
                    beside_a = split(D[d, other, rows, :])
                    beside_r = split(R[d, other, rows, :])
                    near_x = [beside_a[j] + source[j] * beside_r[j] for j in range(tiles)]
                    own_a = split(D[d, own, rows, :])
                    inverse = split(R[d, own, rows, :])
                    field = [own_a[j] + own_source[j] * inverse[j] for j in range(tiles)]
                    near = stream(forward_y, pair % 2 == 0, pair, rows, field, near_x)
                    value = [near[j] * inverse[j] for j in range(tiles)]
                    out[d, x, rows, :] = join(value)
                    excess = split(PV[d, x, rows, :])
                    excess = [excess[j] - warm[j] for j in range(tiles)]
                    part_g = [(field[j] + value[j]) * excess[j] for j in range(tiles)]
                    part_e = [inverse[j] * excess[j] for j in range(tiles)]
                    total_g = part_g if pair == 0 else [total_g[j] + part_g[j] for j in range(tiles)]
                    total_e = part_e if pair == 0 else [total_e[j] + part_e[j] for j in range(tiles)]
                SUMG[x, rows, :] = SUMG[x, rows, :] + join(total_g)
                SUMP[x, rows, :] = SUMP[x, rows, :] + join(total_e)

        def sweep(step, forward_y, hooks):
            def layer(i, carry):
                for at, hook in hooks["before"].items():
                    pl.when(i == at)(hook)
                for side in range(2):
                    x = i if side == 0 else last - i
                    (slab_b if step else slab_a)(forward_y, side, x)
                for at, hook in hooks["after"].items():
                    pl.when(i == at)(hook)
                return carry

            lax.fori_loop(0, nx, layer, 0)

        def both(step, hooks):
            @pl.when(ahead)
            def _():
                sweep(step, True, hooks)

            @pl.when(jnp.logical_not(ahead))
            def _():
                sweep(step, False, hooks)

        def set_source(x, slot, row):
            WS[slot] = wide_weight * row

        def wait_halo0():
            with jax.named_scope("waithalo0"):
                arrive(lambda down: halo(0, down))

        late_down = space == n_space // 2
        late_up = space == n_space // 2 - 1

        def send_halo1():
            @pl.when(jnp.logical_and(has_low, jnp.logical_not(late_down)))
            def _():
                halo(1, True).start()

            @pl.when(jnp.logical_and(has_high, jnp.logical_not(late_up)))
            def _():
                halo(1, False).start()

        def send_halo1_late():
            @pl.when(late_down)
            def _():
                halo(1, True).start()

            @pl.when(late_up)
            def _():
                halo(1, False).start()

        def middle0():
            with jax.named_scope("middle0"):
                exchange_middle(0)

        with jax.named_scope("sweepA"):
            both(0, {"before": {last: wait_halo0}, "after": {0: send_halo1, MIDDLE0: middle0}})
        with jax.named_scope("fold1"):
            for x in range(nx):
                fold(1, 0, x, BASE[x] * SUMA[x])
                fold(1, 1, x, BASE[x] * wide_weight * SUMR[x])
            exchange_start(1)

        with jax.named_scope("halodiag"):
            arrive(lambda down: rows_copy(0, down))

            def halo_diagonal(way):
                own = nx if way == 0 else 0
                for j in range(tiles):
                    base = base_of(HR[way, 1, :, cuts[j]], j)
                    rate = base * (0.2 + 0.8 * HR[way, 0, :, cuts[j]])
                    for pair in range(half):
                        R[pair + way * half, own, :, cuts[j]] = reciprocal(CF[pair, 5] + rate)

            @pl.when(has_high)
            def _():
                halo_diagonal(0)

            @pl.when(has_low)
            def _():
                halo_diagonal(1)

        with jax.named_scope("end0"):
            coupling, temperature = exchange_end(0)
        send_halo1_late()
        with jax.named_scope("source0"):
            cell_source = NDIR * NB * owv[...]
            first_source = coupling + cell_source
            for x in range(nx):
                SV[x] = first_source[x : x + 1]
            start(lambda down: rows_copy(1, down))
            for x in range(nx):
                WS[x + 1] = wide_weight * first_source[x : x + 1]
                TB[x] = jnp.broadcast_to(temperature[x : x + 1], (SUB, plane))

        def wait_halo1():
            with jax.named_scope("waithalo1"):
                arrive(lambda down: halo(1, down))
                arrive(lambda down: rows_copy(1, down))

                @pl.when(has_high)
                def _():
                    WS[nx + 1] = wide_weight * SH[0]

                @pl.when(jnp.logical_not(has_high))
                def _():
                    WS[nx + 1] = jnp.zeros((nbands, plane), jnp.float32)

                @pl.when(has_low)
                def _():
                    WS[0] = wide_weight * SH[1]

                @pl.when(jnp.logical_not(has_low))
                def _():
                    WS[0] = jnp.zeros((nbands, plane), jnp.float32)

        def middle1():
            with jax.named_scope("middle1"):
                exchange_middle(1)

        with jax.named_scope("sweepB"):
            both(1, {"before": {last: wait_halo1}, "after": {MIDDLE1: middle1}})
        with jax.named_scope("end1"):
            first, second = exchange_end(1)
        with jax.named_scope("fold2"):
            scale = 0.2 + 0.8 * denv[...]
            second_source = scale * (first + first_source * second) + cell_source
            for x in range(nx):
                source = wide_weight * second_source[x : x + 1]
                WS[x + 1] = source
                fold(2, 0, x, 0.8 * BASE[x] * (SUMG[x] + source * SUMP[x]))
            exchange_start(2)

        with jax.named_scope("final"):

            def finish(x, carry):
                source = WS[x + 1]
                for d in range(ndir):
                    out[d, x] = out[d, x] + source * R[d, x + (0 if d < half else 1)]
                return carry

            lax.fori_loop(0, nx, finish, 0)
        with jax.named_scope("exch2"):
            exchange_middle(2)
            grad[...] = exchange_end(2)[0] * (-0.125 / ITERS)
        with jax.named_scope("drain"):
            for n in range(3):
                exchange_drain(n)
            for step in range(2):
                drain(lambda down: halo(step, down))
                drain(lambda down: rows_copy(step, down))

    return kernel


def solution(mesh):
    n_space, n_dir, n_band = mesh.shape["space"], mesh.shape["dir"], mesh.shape["band"]
    placed = (
        P("dir", "band", "space", None),
        P("dir", "band", "space", None),
        P("space", None),
        P("space", None),
        P(None, "band"),
        P("band"),
        P(),
        P("space", None),
    )

    def on_device(adj, pri, den, mat, rt, gs, hc, ow):
        ndir, nbands, nx, plane = adj.shape
        half = ndir // 2
        f32 = jnp.float32
        vmem = lambda *shape: pltpu.VMEM(shape, f32)
        dma = pltpu.SemaphoreType.DMA
        call = pl.pallas_call(
            make_kernel(ndir, nbands, nx, plane, n_space, n_dir, n_band),
            out_shape=(
                jax.ShapeDtypeStruct((ndir, nx, nbands, plane), f32),
                jax.ShapeDtypeStruct((nx, plane), f32),
            ),
            in_specs=[pl.BlockSpec(memory_space=pltpu.HBM)] * 8,
            out_specs=(pl.BlockSpec(memory_space=pltpu.VMEM),) * 2,
            scratch_shapes=[
                vmem(ndir, nx + 1, nbands, plane),
                vmem(ndir, nx, nbands, plane),
                vmem(ndir, nx + 1, nbands, plane),
                vmem(ndir, nx + 1, nbands, plane),
                vmem(nx, nbands, plane),
                vmem(nx, nbands, plane),
                vmem(nx + 2, nbands, plane),
                vmem(half, 6, nbands, LANES),
                vmem(nx, nbands, plane),
                vmem(nx, nbands, plane),
                vmem(nx, nbands, plane),
                vmem(nx, nbands, plane),
                vmem(nx, SUB, plane),
                vmem(nx, 1, plane),
                vmem(2, 1, plane),
                vmem(2, 2, 1, plane),
                vmem(2, 2, 1, plane),
                vmem(nx, plane),
                pltpu.VMEM((nx, plane), jnp.int32),
                vmem(*rt.shape),
                vmem(1, nbands),
                vmem(1, NB),
                vmem(nx, plane),
                vmem(3, n_dir, 2, nx, plane),
                vmem(3, n_band, 2, nx, plane),
                dma((2, 4)),
                dma((6,)),
                dma((2, 2)),
                dma((2, 2)),
                dma((2, 2)),
                dma((2, 2)),
                dma((3, n_dir - 1)),
                dma((3, n_dir - 1)),
                dma((3,)),
                dma((3,)),
            ],
            compiler_params=pltpu.CompilerParams(
                collective_id=0, has_side_effects=True, vmem_limit_bytes=40 * 1024 * 1024
            ),
        )
        turn = lambda v: jnp.transpose(v, (0, 2, 1, 3))
        operands = (
            turn(adj), turn(pri), den, mat, rt, gs.reshape(1, nbands), hc.reshape(1, NB), ow
        )
        dual, grad = call(*[pltpu.with_memory_space_constraint(v, pltpu.HBM) for v in operands])
        return turn(dual), grad

    return jax.shard_map(
        on_device,
        mesh=mesh,
        in_specs=placed,
        out_specs=(P("dir", "band", "space", None), P("space", None)),
        check_vma=False,
    )
```

```python
import jax
import jax.numpy as jnp
import numpy as np
from jax import lax
from jax.experimental import pallas as pl
from jax.experimental.pallas import tpu as pltpu
from jax.sharding import PartitionSpec as P

NDIR = 64
NB = 32
NY = 192
ITERS = 2
LANES = 128
SUB = 8
SECOND = 2
THIRD = 3
LAST = 4
MIDDLE0 = 3
MIDDLET = 0
MIDDLE1 = 2
MESH = pl.DeviceIdType.MESH


def direction_constants(half, blocks):
    index = np.arange(blocks * half, dtype=np.float32)
    azimuth = np.float32(np.pi) * (index + np.float32(0.5)) / np.float32(NDIR // 2)
    azimuth = azimuth - np.float32(np.pi / 2)
    pair = np.arange(blocks * half) % half
    along_z = np.float32(0.4) * (1 - 2 * (pair % 2)).astype(np.float32)
    tilt = np.sqrt(np.float32(1.0) - along_z * along_z)
    along_x = np.abs(tilt * np.cos(azimuth))
    along_y = np.abs(tilt * np.sin(azimuth))
    return (
        along_x.reshape(blocks, half),
        along_y.reshape(blocks, half),
        np.abs(along_z).reshape(blocks, half),
    )


def by_block(block, values):
    chosen = jnp.float32(values[-1])
    for index in range(len(values) - 2, -1, -1):
        chosen = jnp.where(block == index, jnp.float32(values[index]), chosen)
    return chosen


def make_kernel(ndir, nbands, nx, plane, n_space, n_dir, n_band):
    half = ndir // 2
    tiles = plane // LANES
    subs = nbands // SUB
    last = nx - 1
    const_x, const_y, const_z = direction_constants(half, n_dir)

    def kernel(
        adj, pri, den, mat, rt, gs, hc, ow,
        out, grad,
        A, PV, D, R, RATE, BASE, WS, CF, SUMA, SUMP, SUMR, SUMG, TB, SV, SH, HS, HR,
        denv, matv, rtv, gsv, hcv, owv, TL,
        XB, ZB,
        load_sem, small_sem, h_send, h_recv, r_send, r_recv, x_send, x_recv, z_send, z_recv,
    ):
        space = lax.axis_index("space")
        block = lax.axis_index("dir")
        band = lax.axis_index("band")
        other_band = 1 - band
        has_low = space > 0
        has_high = space < n_space - 1

        barrier = pltpu.get_barrier_semaphore()
        for k in range(1, n_dir):
            peer = lax.rem(block + k, n_dir)
            pl.semaphore_signal(barrier, inc=1, device_id={"dir": peer}, device_id_type=MESH)
        before, after = lax.rem(block + n_dir - 1, n_dir), lax.rem(block + 1, n_dir)
        pl.semaphore_signal(barrier, inc=1, device_id={"band": other_band}, device_id_type=MESH)
        shared = jnp.logical_or(space < 2, space >= n_space - 2)

        @pl.when(shared)
        def _():
            pl.semaphore_signal(
                barrier, inc=1, device_id={"dir": after, "band": other_band}, device_id_type=MESH
            )

        @pl.when(has_low)
        def _():
            pl.semaphore_signal(barrier, inc=1, device_id={"space": space - 1}, device_id_type=MESH)

        @pl.when(has_high)
        def _():
            pl.semaphore_signal(barrier, inc=1, device_id={"space": space + 1}, device_id_type=MESH)

        smalls = [
            pltpu.make_async_copy(src, dst, small_sem.at[i])
            for i, (src, dst) in enumerate(
                ((den, denv), (mat, matv), (rt, rtv), (gs, gsv), (hc, hcv), (ow, owv))
            )
        ]
        group = 4
        loads_a = []
        loads_p = []
        for g in range(ndir // group):
            first = g * group
            shift = 0 if first < half else 1
            loads_a.append(
                pltpu.make_async_copy(
                    adj.at[pl.ds(first, group)],
                    A.at[pl.ds(first, group), pl.ds(shift, nx)],
                    load_sem.at[0, g],
                )
            )
            loads_p.append(
                pltpu.make_async_copy(
                    pri.at[pl.ds(first, group)], PV.at[pl.ds(first, group)], load_sem.at[1, g]
                )
            )
        for copy in smalls:
            copy.start()

        def beside(src, dst, down, send_sem, recv_sem):
            return pltpu.make_async_remote_copy(
                src_ref=src,
                dst_ref=dst,
                send_sem=send_sem,
                recv_sem=recv_sem,
                device_id={"space": space - 1 if down else space + 1},
                device_id_type=MESH,
            )

        def halo(step, down):
            way = 0 if down else 1
            rows = pl.ds(0 if down else half, half)
            buffer = D if step else A
            if step:
                src = D.at[rows, 0 if down else nx]
            else:
                src = adj.at[rows, 0 if down else last]
            dst = buffer.at[rows, nx if down else 0]
            return beside(src, dst, down, h_send.at[step, way], h_recv.at[step, way])

        def rows_copy(step, down):
            way = 0 if down else 1
            if step == 0:
                src, dst = HS.at[way], HR.at[way]
            else:
                src, dst = SV.at[0 if down else last], SH.at[way]
            return beside(src, dst, down, r_send.at[step, way], r_recv.at[step, way])

        def both_ways(make, act, receive=False):
            @pl.when(has_high if receive else has_low)
            def _():
                act(make(True))

            @pl.when(has_low if receive else has_high)
            def _():
                act(make(False))

        def start(make):
            both_ways(make, lambda copy: copy.start())

        def arrive(make):
            both_ways(make, lambda copy: copy.wait_recv(), receive=True)

        def drain(make):
            both_ways(make, lambda copy: copy.wait_send())

        @pl.when(jnp.logical_not(has_high))
        def _():
            def clear(d, carry):
                for buffer in (A, D):
                    buffer[d, nx] = jnp.zeros((nbands, plane), jnp.float32)
                R[d, nx + 1] = jnp.zeros((nbands, plane), jnp.float32)
                return carry

            lax.fori_loop(0, half, clear, 0)

        @pl.when(jnp.logical_not(has_low))
        def _():
            def clear(d, carry):
                for buffer in (A, D):
                    buffer[half + d, 0] = jnp.zeros((nbands, plane), jnp.float32)
                R[d, 0] = jnp.zeros((nbands, plane), jnp.float32)
                return carry

            lax.fori_loop(0, half, clear, 0)

        with jax.named_scope("smallwait"):
            for copy in smalls:
                copy.wait()
            for copy in loads_a:
                copy.start()
            for copy in loads_p:
                copy.start()
        with jax.named_scope("tables"):
            for way, x in ((0, 0), (1, last)):
                HS[way, 0] = denv[x : x + 1, :]
                HS[way, 1] = matv[x : x + 1, :].astype(jnp.float32)
            row_index = lax.broadcasted_iota(jnp.int32, (nbands, nbands), 0)
            lane_index = lax.broadcasted_iota(jnp.int32, (nbands, nbands), 1)

            def column(row):
                spread = jnp.where(row_index == lane_index, row, 0.0)
                return jnp.broadcast_to(jnp.sum(spread, axis=1, keepdims=True), (nbands, LANES))

            rates = [column(rtv[m : m + 1, :]) for m in range(rt.shape[0])]
            speed = column(gsv[...])
            heat = hcv[...]
            total_heat = jnp.sum(heat, axis=1, keepdims=True)
            wide_row = lax.broadcasted_iota(jnp.int32, (nbands, NB), 0) + band * nbands
            wide_lane = lax.broadcasted_iota(jnp.int32, (nbands, NB), 1)
            local_heat = jnp.sum(jnp.where(wide_row == wide_lane, heat, 0.0), axis=1, keepdims=True)
            weight = jnp.broadcast_to(local_heat / (NDIR * total_heat), (nbands, LANES))
            wide_weight = jnp.concatenate([weight] * tiles, axis=1)
            mean_scale = 1.0 / (ndir * jnp.sum(weight, axis=0, keepdims=True))
            lane = lax.broadcasted_iota(jnp.int32, (nbands, LANES), 1)
            ahead = block >= n_dir // 2
            middle = jnp.where(ahead, 63, 64)
            edge = jnp.where(ahead, LANES - 1, 0)
            for pair in range(half):
                sx = speed * by_block(block, const_x[:, pair])
                sy = speed * by_block(block, const_y[:, pair])
                sz = speed * jnp.float32(const_z[0, pair])
                CF[pair, 0] = sx
                CF[pair, 1] = sy
                CF[pair, 2] = jnp.where(lane == middle, 0.0, sy)
                CF[pair, 3] = jnp.where(lane == edge, 0.0, sy)
                CF[pair, 4] = sz
                CF[pair, 5] = sx + sy + sz

            def base_of(kind_row, j):
                kind = jnp.broadcast_to(kind_row, (nbands, LANES))
                base = rates[-1]
                for m in range(rt.shape[0] - 2, -1, -1):
                    base = jnp.where(kind == m, rates[m], base)
                return base

            cuts = [slice(j * LANES, (j + 1) * LANES) for j in range(tiles)]
            for x in range(nx):
                for j in range(tiles):
                    base = base_of(matv[x : x + 1, cuts[j]], j)
                    BASE[x, :, cuts[j]] = base
                    RATE[x, :, cuts[j]] = base * (0.2 + 0.8 * denv[x : x + 1, cuts[j]])

        def reciprocal(diagonal):
            guess = pl.reciprocal(diagonal, approx=True)
            return guess * (2.0 - diagonal * guess)

        with jax.named_scope("diagonal"):

            def diagonals(x, carry):
                for s in range(subs):
                    rows = pl.ds(s * SUB, SUB)
                    rate = RATE[x, rows, :]
                    total = None
                    for pair in range(half):
                        csum = jnp.concatenate([CF[pair, 5, rows, :]] * tiles, axis=1)
                        inverse = reciprocal(csum + rate)
                        R[pair, x + 1, rows, :] = inverse
                        total = inverse if pair == 0 else total + inverse
                    SUMR[x, rows, :] = total + total
                return carry

            lax.fori_loop(0, nx, diagonals, 0)

        with jax.named_scope("barrier"):
            most = jnp.logical_or(space == 1, space == n_space - 2)

            @pl.when(most)
            def _():
                pl.semaphore_wait(barrier, n_dir + 3)

            @pl.when(jnp.logical_not(most))
            def _():
                pl.semaphore_wait(barrier, n_dir + 2)

        with jax.named_scope("halo0"):
            start(lambda down: halo(0, down))

        start(lambda down: rows_copy(0, down))

        def sum_group(source, target, g, shift):
            def body(x, carry):
                total = source[g * group, x + shift]
                for d in range(1, group):
                    total = total + source[g * group + d, x + shift]
                if g:
                    total = total + target[x]
                target[x] = total
                return carry

            lax.fori_loop(0, nx, body, 0)

        def x_copy(n, k):
            ref = XB.at[n, block]
            return pltpu.make_async_remote_copy(
                src_ref=ref,
                dst_ref=ref,
                send_sem=x_send.at[n, k - 1],
                recv_sem=x_recv.at[n, k - 1],
                device_id={"dir": lax.rem(block + k, n_dir)},
                device_id_type=MESH,
            )

        def z_copy(n, aside=False):
            ref = ZB.at[n, band]
            return pltpu.make_async_remote_copy(
                src_ref=ref,
                dst_ref=ref,
                send_sem=z_send.at[n],
                recv_sem=z_recv.at[n],
                device_id={"dir": before if aside else block, "band": other_band},
                device_id_type=MESH,
            )

        def x_start(n):
            for k in range(1, n_dir):
                x_copy(n, k).start()

        def x_end(n):
            for k in range(1, n_dir):
                x_copy(n, k).wait_recv()
            total = XB[n, 0]
            for k in range(1, n_dir):
                total = total + XB[n, k]
            return total

        def x_then_z(n):
            ZB[n, band] = x_end(n)
            if n == LAST:
                z_copy(n).start()
            else:

                @pl.when(shared)
                def _():
                    z_copy(n, True).start()

                @pl.when(jnp.logical_not(shared))
                def _():
                    z_copy(n).start()

        def exchange_end(n):
            z_copy(n).wait_recv()
            return ZB[n, 0] + ZB[n, 1]

        def exchange_drain(n):
            for k in range(1, n_dir):
                x_copy(n, k).wait_send()
            z_copy(n).wait_send()

        def folded(value):
            return jnp.sum(value, axis=0, keepdims=True)

        with jax.named_scope("sum_a"):
            for g in range(ndir // group):
                loads_a[g].wait()
                sum_group(A, SUMA, g, 0 if g * group < half else 1)
            for x in range(nx):
                XB[0, block, x : x + 1, :] = folded(RATE[x] * SUMA[x])
            x_start(0)
            for x in range(nx):
                XB[THIRD, block, x : x + 1, :] = folded(BASE[x] * wide_weight * SUMR[x])
            x_start(THIRD)
        with jax.named_scope("sum_p"):
            for g in range(ndir // group):
                loads_p[g].wait()
                sum_group(PV, SUMP, g, 0)
            for x in range(nx):
                share = folded(wide_weight * SUMP[x])
                XB[1, block, x : x + 1, :] = share
                TL[x : x + 1, :] = share * mean_scale[:, :1]
                TB[x] = jnp.broadcast_to(TL[x : x + 1, :], (SUB, plane))
            x_start(1)

        for x in range(nx):
            for buffer in (SUMA, SUMP, SUMG):
                buffer[x] = jnp.zeros((nbands, plane), jnp.float32)

        lane8 = lax.broadcasted_iota(jnp.int32, (SUB, LANES), 1)
        low_lanes = lane8 < LANES // 2
        edge_first = lane8 == 0
        edge_last = lane8 == LANES - 1

        def stream(forward_y, up_z, pair, rows, field, near_x):
            cx = CF[pair, 0, rows, :]
            cy = [CF[pair, 1 + i, rows, :] for i in range(3)]
            cz = CF[pair, 4, rows, :]
            turn = [pltpu.roll(v, LANES - 1 if forward_y else 1, 1) for v in field]
            halfway = [pltpu.roll(v, LANES // 2, 1) for v in field]
            values = []
            for j in range(tiles):
                moved = turn[j]
                if forward_y:
                    coef = cy[(0, 1, 2)[j % 3]]
                    if j % 3 != 2:
                        moved = jnp.where(edge_last, turn[j + 1], moved)
                else:
                    coef = cy[(2, 1, 0)[j % 3]]
                    if j % 3 != 0:
                        moved = jnp.where(edge_first, turn[j - 1], moved)
                value = cx * near_x[j] + coef * moved
                if up_z:
                    if j + 2 < tiles:
                        value = value + cz * jnp.where(low_lanes, halfway[j + 1], halfway[j + 2])
                    elif j + 1 < tiles:
                        value = value + cz * jnp.where(low_lanes, halfway[j + 1], 0.0)
                else:
                    if j >= 2:
                        value = value + cz * jnp.where(low_lanes, halfway[j - 2], halfway[j - 1])
                    elif j >= 1:
                        value = value + cz * jnp.where(low_lanes, 0.0, halfway[j - 1])
                values.append(value)
            return values

        def split(ref_rows):
            return [ref_rows[:, c] for c in cuts]

        def join(parts):
            return jnp.concatenate(parts, axis=1)

        def slab_a(forward_y, side, x):
            for s in range(subs):
                rows = pl.ds(s * SUB, SUB)
                total = None
                for pair in range(half):
                    d = pair + side * half
                    own, other = x + side, x + 1 - side
                    near = stream(
                        forward_y, pair % 2 == 0, pair, rows, split(A[d, own, rows, :]), split(A[d, other, rows, :])
                    )
                    value = join(near) * R[pair, x + 1, rows, :]
                    D[d, own, rows, :] = value
                    total = value if pair == 0 else total + value
                SUMA[x, rows, :] = SUMA[x, rows, :] + total

        def slab_b(forward_y, side, x):
            warm = split(TB[x])
            for s in range(subs):
                rows = pl.ds(s * SUB, SUB)
                source = split(WS[x + 2 - 2 * side, rows, :])
                own_source = split(WS[x + 1, rows, :])
                total_g, total_e, total_h = None, None, None
                for pair in range(half):
                    d = pair + side * half
                    own, other = x + side, x + 1 - side
                    beside_a = split(D[d, other, rows, :])
                    beside_r = split(R[pair, x + 2 - 2 * side, rows, :])
                    near_x = [beside_a[j] + source[j] * beside_r[j] for j in range(tiles)]
                    own_a = split(D[d, own, rows, :])
                    inverse = split(R[pair, x + 1, rows, :])
                    field = [own_a[j] + own_source[j] * inverse[j] for j in range(tiles)]
                    near = stream(forward_y, pair % 2 == 0, pair, rows, field, near_x)
                    value = [near[j] * inverse[j] for j in range(tiles)]
                    out[d, x, rows, :] = join(value)
                    excess = split(PV[d, x, rows, :])
                    excess = [excess[j] - warm[j] for j in range(tiles)]
                    both_duals = [field[j] + value[j] for j in range(tiles)]
                    part_g = [both_duals[j] * excess[j] for j in range(tiles)]
                    part_e = [inverse[j] * excess[j] for j in range(tiles)]
                    total_g = part_g if pair == 0 else [total_g[j] + part_g[j] for j in range(tiles)]
                    total_e = part_e if pair == 0 else [total_e[j] + part_e[j] for j in range(tiles)]
                    total_h = both_duals if pair == 0 else [total_h[j] + both_duals[j] for j in range(tiles)]
                SUMG[x, rows, :] = SUMG[x, rows, :] + join(total_g)
                SUMP[x, rows, :] = SUMP[x, rows, :] + join(total_e)
                SUMA[x, rows, :] = SUMA[x, rows, :] + join(total_h)

        def sweep(step, forward_y, hooks):
            def layer(i, carry):
                for at, hook in hooks["before"].items():
                    pl.when(i == at)(hook)
                for side in range(2):
                    x = i if side == 0 else last - i
                    (slab_b if step else slab_a)(forward_y, side, x)
                for at, hook in hooks["after"].items():
                    pl.when(i == at)(hook)
                return carry

            lax.fori_loop(0, nx, layer, 0)

        def both(step, hooks):
            @pl.when(ahead)
            def _():
                sweep(step, True, hooks)

            @pl.when(jnp.logical_not(ahead))
            def _():
                sweep(step, False, hooks)

        def set_source(x, slot, row):
            WS[slot] = wide_weight * row

        def wait_halo0():
            with jax.named_scope("waithalo0"):
                arrive(lambda down: halo(0, down))

        def send_halo1():
            start(lambda down: halo(1, down))

        def middle0():
            with jax.named_scope("middle0"):
                x_then_z(0)

        def middle_t():
            with jax.named_scope("middleT"):
                x_then_z(THIRD)
                x_then_z(1)

        with jax.named_scope("sweepA"):
            both(0, {"before": {last: wait_halo0}, "after": {0: send_halo1, MIDDLE0: middle0}})
        with jax.named_scope("fold1"):
            for x in range(nx):
                XB[SECOND, block, x : x + 1, :] = folded(BASE[x] * SUMA[x])
                SUMA[x] = jnp.zeros((nbands, plane), jnp.float32)
            x_start(SECOND)

        with jax.named_scope("halodiag"):
            arrive(lambda down: rows_copy(0, down))

            def halo_diagonal(way):
                own = nx + 1 if way == 0 else 0
                for j in range(tiles):
                    base = base_of(HR[way, 1, :, cuts[j]], j)
                    rate = base * (0.2 + 0.8 * HR[way, 0, :, cuts[j]])
                    for pair in range(half):
                        R[pair, own, :, cuts[j]] = reciprocal(CF[pair, 5] + rate)

            @pl.when(has_high)
            def _():
                halo_diagonal(0)

            @pl.when(has_low)
            def _():
                halo_diagonal(1)

        with jax.named_scope("end0"):
            coupling = exchange_end(0)
        with jax.named_scope("source0"):
            cell_source = NDIR * NB * owv[...]
            first_source = coupling + cell_source
            for x in range(nx):
                SV[x] = first_source[x : x + 1]
            start(lambda down: rows_copy(1, down))
        with jax.named_scope("source1"):
            for x in range(nx):
                source = wide_weight * first_source[x : x + 1]
                WS[x + 1] = source

        def wait_halo1():
            with jax.named_scope("waithalo1"):
                arrive(lambda down: halo(1, down))
                arrive(lambda down: rows_copy(1, down))

                @pl.when(has_high)
                def _():
                    WS[nx + 1] = wide_weight * SH[0]

                @pl.when(jnp.logical_not(has_high))
                def _():
                    WS[nx + 1] = jnp.zeros((nbands, plane), jnp.float32)

                @pl.when(has_low)
                def _():
                    WS[0] = wide_weight * SH[1]

                @pl.when(jnp.logical_not(has_low))
                def _():
                    WS[0] = jnp.zeros((nbands, plane), jnp.float32)

        def middle1():
            with jax.named_scope("middle1"):
                x_then_z(SECOND)

        with jax.named_scope("sweepB"):
            both(1, {"before": {last: wait_halo1}, "after": {MIDDLET: middle_t, MIDDLE1: middle1}})
        with jax.named_scope("end1"):
            first_source = SV[:, 0]
            total = exchange_end(SECOND) + first_source * exchange_end(THIRD)
            temperature = exchange_end(1)
            shift = temperature - TL[...]
        with jax.named_scope("fold2"):
            scale = 0.2 + 0.8 * denv[...]
            second_source = scale * total + NDIR * NB * owv[...]
            for x in range(nx):
                source = wide_weight * second_source[x : x + 1]
                WS[x + 1] = source
                XB[LAST, block, x : x + 1, :] = folded(
                    0.8
                    * BASE[x]
                    * (SUMG[x] + source * SUMP[x] - shift[x : x + 1] * (SUMA[x] + source * SUMR[x]))
                )
            x_start(LAST)

        with jax.named_scope("final"):

            def finish(x, carry):
                source = WS[x + 1]
                for d in range(ndir):
                    out[d, x] = out[d, x] + source * R[d % half, x + 1]
                return carry

            lax.fori_loop(0, nx, finish, 0)
        with jax.named_scope("exch2"):
            with jax.named_scope("last_x"):
                x_then_z(LAST)
            with jax.named_scope("last_z"):
                grad[...] = exchange_end(LAST) * (-0.125 / ITERS)
        with jax.named_scope("drain"):
            for n in range(5):
                exchange_drain(n)
            for step in range(2):
                drain(lambda down: halo(step, down))
                drain(lambda down: rows_copy(step, down))

    return kernel


def solution(mesh):
    n_space, n_dir, n_band = mesh.shape["space"], mesh.shape["dir"], mesh.shape["band"]
    placed = (
        P("dir", "band", "space", None),
        P("dir", "band", "space", None),
        P("space", None),
        P("space", None),
        P(None, "band"),
        P("band"),
        P(),
        P("space", None),
    )

    def on_device(adj, pri, den, mat, rt, gs, hc, ow):
        ndir, nbands, nx, plane = adj.shape
        half = ndir // 2
        f32 = jnp.float32
        vmem = lambda *shape: pltpu.VMEM(shape, f32)
        dma = pltpu.SemaphoreType.DMA
        call = pl.pallas_call(
            make_kernel(ndir, nbands, nx, plane, n_space, n_dir, n_band),
            out_shape=(
                jax.ShapeDtypeStruct((ndir, nx, nbands, plane), f32),
                jax.ShapeDtypeStruct((nx, plane), f32),
            ),
            in_specs=[pl.BlockSpec(memory_space=pltpu.HBM)] * 8,
            out_specs=(pl.BlockSpec(memory_space=pltpu.VMEM),) * 2,
            scratch_shapes=[
                vmem(ndir, nx + 1, nbands, plane),
                vmem(ndir, nx, nbands, plane),
                vmem(ndir, nx + 1, nbands, plane),
                vmem(half, nx + 2, nbands, plane),
                vmem(nx, nbands, plane),
                vmem(nx, nbands, plane),
                vmem(nx + 2, nbands, plane),
                vmem(half, 6, nbands, LANES),
                vmem(nx, nbands, plane),
                vmem(nx, nbands, plane),
                vmem(nx, nbands, plane),
                vmem(nx, nbands, plane),
                vmem(nx, SUB, plane),
                vmem(nx, 1, plane),
                vmem(2, 1, plane),
                vmem(2, 2, 1, plane),
                vmem(2, 2, 1, plane),
                vmem(nx, plane),
                pltpu.VMEM((nx, plane), jnp.int32),
                vmem(*rt.shape),
                vmem(1, nbands),
                vmem(1, NB),
                vmem(nx, plane),
                vmem(nx, plane),
                vmem(5, n_dir, nx, plane),
                vmem(5, n_band, nx, plane),
                dma((2, 4)),
                dma((6,)),
                dma((2, 2)),
                dma((2, 2)),
                dma((2, 2)),
                dma((2, 2)),
                dma((5, n_dir - 1)),
                dma((5, n_dir - 1)),
                dma((5,)),
                dma((5,)),
            ],
            compiler_params=pltpu.CompilerParams(
                collective_id=0, has_side_effects=True, vmem_limit_bytes=40 * 1024 * 1024
            ),
        )
        turn = lambda v: jnp.transpose(v, (0, 2, 1, 3))
        operands = (
            turn(adj), turn(pri), den, mat, rt, gs.reshape(1, nbands), hc.reshape(1, NB), ow
        )
        dual, grad = call(*[pltpu.with_memory_space_constraint(v, pltpu.HBM) for v in operands])
        return turn(dual), grad

    return jax.shard_map(
        on_device,
        mesh=mesh,
        in_specs=placed,
        out_specs=(P("dir", "band", "space", None), P("space", None)),
        check_vma=False,
    )
```

```python
import jax
import jax.numpy as jnp
import numpy as np
from jax import lax
from jax.experimental import pallas as pl
from jax.experimental.pallas import tpu as pltpu
from jax.sharding import PartitionSpec as P

NDIR = 64
NB = 32
NY = 192
ITERS = 2
LANES = 128
SUB = 8
SECOND = 2
THIRD = 3
EARLY = 4
LATE = 5
MIDDLE0 = 3
MIDDLE1 = 2
MESH = pl.DeviceIdType.MESH


def direction_constants(half, blocks):
    index = np.arange(blocks * half, dtype=np.float32)
    azimuth = np.float32(np.pi) * (index + np.float32(0.5)) / np.float32(NDIR // 2)
    azimuth = azimuth - np.float32(np.pi / 2)
    pair = np.arange(blocks * half) % half
    along_z = np.float32(0.4) * (1 - 2 * (pair % 2)).astype(np.float32)
    tilt = np.sqrt(np.float32(1.0) - along_z * along_z)
    along_x = np.abs(tilt * np.cos(azimuth))
    along_y = np.abs(tilt * np.sin(azimuth))
    return (
        along_x.reshape(blocks, half),
        along_y.reshape(blocks, half),
        np.abs(along_z).reshape(blocks, half),
    )


def by_block(block, values):
    chosen = jnp.float32(values[-1])
    for index in range(len(values) - 2, -1, -1):
        chosen = jnp.where(block == index, jnp.float32(values[index]), chosen)
    return chosen


def make_kernel(ndir, nbands, nx, plane, n_space, n_dir, n_band):
    half = ndir // 2
    tiles = plane // LANES
    subs = nbands // SUB
    last = nx - 1
    const_x, const_y, const_z = direction_constants(half, n_dir)

    def kernel(
        adj, pri, den, mat, rt, gs, hc, ow,
        out, grad,
        A, PV, D, R, RATE, BASE, WS, CF, SUMA, SUMP, SUMR, SUMG, TB, SV, SH, HS, HR,
        denv, matv, rtv, gsv, hcv, owv, TL, SH_T,
        XB, ZB, XE, XL, ZE, ZL,
        load_sem, small_sem, h_send, h_recv, r_send, r_recv, x_send, x_recv, z_send, z_recv,
    ):
        space = lax.axis_index("space")
        block = lax.axis_index("dir")
        band = lax.axis_index("band")
        other_band = 1 - band
        odd = lax.rem(space, 2)
        has_low = space > 0
        has_high = space < n_space - 1

        barrier = pltpu.get_barrier_semaphore()
        for k in range(1, n_dir):
            peer = lax.rem(block + k, n_dir)
            pl.semaphore_signal(barrier, inc=1, device_id={"dir": peer}, device_id_type=MESH)
        before, after = lax.rem(block + n_dir - 1, n_dir), lax.rem(block + 1, n_dir)
        pl.semaphore_signal(barrier, inc=1, device_id={"band": other_band}, device_id_type=MESH)
        shared = jnp.logical_or(space < 2, space >= n_space - 2)

        @pl.when(shared)
        def _():
            pl.semaphore_signal(
                barrier, inc=1, device_id={"dir": after, "band": other_band}, device_id_type=MESH
            )

        @pl.when(has_low)
        def _():
            pl.semaphore_signal(barrier, inc=1, device_id={"space": space - 1}, device_id_type=MESH)

        @pl.when(has_high)
        def _():
            pl.semaphore_signal(barrier, inc=1, device_id={"space": space + 1}, device_id_type=MESH)

        smalls = [
            pltpu.make_async_copy(src, dst, small_sem.at[i])
            for i, (src, dst) in enumerate(
                ((den, denv), (mat, matv), (rt, rtv), (gs, gsv), (hc, hcv), (ow, owv))
            )
        ]
        group = 4
        loads_a = []
        loads_p = []
        for g in range(ndir // group):
            first = g * group
            shift = 0 if first < half else 1
            loads_a.append(
                pltpu.make_async_copy(
                    adj.at[pl.ds(first, group)],
                    A.at[pl.ds(first, group), pl.ds(shift, nx)],
                    load_sem.at[0, g],
                )
            )
            loads_p.append(
                pltpu.make_async_copy(
                    pri.at[pl.ds(first, group)], PV.at[pl.ds(first, group)], load_sem.at[1, g]
                )
            )
        for copy in smalls:
            copy.start()

        def beside(src, dst, down, send_sem, recv_sem):
            return pltpu.make_async_remote_copy(
                src_ref=src,
                dst_ref=dst,
                send_sem=send_sem,
                recv_sem=recv_sem,
                device_id={"space": space - 1 if down else space + 1},
                device_id_type=MESH,
            )

        def halo(step, down):
            way = 0 if down else 1
            rows = pl.ds(0 if down else half, half)
            buffer = D if step else A
            if step:
                src = D.at[rows, 0 if down else nx]
            else:
                src = adj.at[rows, 0 if down else last]
            dst = buffer.at[rows, nx if down else 0]
            return beside(src, dst, down, h_send.at[step, way], h_recv.at[step, way])

        def rows_copy(step, down):
            way = 0 if down else 1
            if step == 0:
                src, dst = HS.at[way], HR.at[way]
            else:
                src, dst = SV.at[0 if down else last], SH.at[way]
            return beside(src, dst, down, r_send.at[step, way], r_recv.at[step, way])

        def both_ways(make, act, receive=False):
            @pl.when(has_high if receive else has_low)
            def _():
                act(make(True))

            @pl.when(has_low if receive else has_high)
            def _():
                act(make(False))

        def start(make):
            @pl.when(jnp.logical_and(has_high, odd == 1))
            def _():
                make(False).start()

            @pl.when(has_low)
            def _():
                make(True).start()

            @pl.when(jnp.logical_and(has_high, odd == 0))
            def _():
                make(False).start()

        def arrive(make):
            both_ways(make, lambda copy: copy.wait_recv(), receive=True)

        def drain(make):
            both_ways(make, lambda copy: copy.wait_send())

        @pl.when(jnp.logical_not(has_high))
        def _():
            def clear(d, carry):
                for buffer in (A, D):
                    buffer[d, nx] = jnp.zeros((nbands, plane), jnp.float32)
                R[d, nx + 1] = jnp.zeros((nbands, plane), jnp.float32)
                return carry

            lax.fori_loop(0, half, clear, 0)

        @pl.when(jnp.logical_not(has_low))
        def _():
            def clear(d, carry):
                for buffer in (A, D):
                    buffer[half + d, 0] = jnp.zeros((nbands, plane), jnp.float32)
                R[d, 0] = jnp.zeros((nbands, plane), jnp.float32)
                return carry

            lax.fori_loop(0, half, clear, 0)

        with jax.named_scope("smallwait"):
            for copy in smalls:
                copy.wait()
            for copy in loads_a:
                copy.start()
            for copy in loads_p:
                copy.start()
        with jax.named_scope("tables"):
            for way, x in ((0, 0), (1, last)):
                HS[way, 0] = denv[x : x + 1, :]
                HS[way, 1] = matv[x : x + 1, :].astype(jnp.float32)
            row_index = lax.broadcasted_iota(jnp.int32, (nbands, nbands), 0)
            lane_index = lax.broadcasted_iota(jnp.int32, (nbands, nbands), 1)

            def column(row):
                spread = jnp.where(row_index == lane_index, row, 0.0)
                return jnp.broadcast_to(jnp.sum(spread, axis=1, keepdims=True), (nbands, LANES))

            rates = [column(rtv[m : m + 1, :]) for m in range(rt.shape[0])]
            speed = column(gsv[...])
            heat = hcv[...]
            total_heat = jnp.sum(heat, axis=1, keepdims=True)
            wide_row = lax.broadcasted_iota(jnp.int32, (nbands, NB), 0) + band * nbands
            wide_lane = lax.broadcasted_iota(jnp.int32, (nbands, NB), 1)
            local_heat = jnp.sum(jnp.where(wide_row == wide_lane, heat, 0.0), axis=1, keepdims=True)
            weight = jnp.broadcast_to(local_heat / (NDIR * total_heat), (nbands, LANES))
            wide_weight = jnp.concatenate([weight] * tiles, axis=1)
            mean_scale = 1.0 / (ndir * jnp.sum(weight, axis=0, keepdims=True))
            lane = lax.broadcasted_iota(jnp.int32, (nbands, LANES), 1)
            ahead = block >= n_dir // 2
            middle = jnp.where(ahead, 63, 64)
            edge = jnp.where(ahead, LANES - 1, 0)
            for pair in range(half):
                sx = speed * by_block(block, const_x[:, pair])
                sy = speed * by_block(block, const_y[:, pair])
                sz = speed * jnp.float32(const_z[0, pair])
                CF[pair, 0] = sx
                CF[pair, 1] = sy
                CF[pair, 2] = jnp.where(lane == middle, 0.0, sy)
                CF[pair, 3] = jnp.where(lane == edge, 0.0, sy)
                CF[pair, 4] = sz
                CF[pair, 5] = sx + sy + sz

            def base_of(kind_row, j):
                kind = jnp.broadcast_to(kind_row, (nbands, LANES))
                base = rates[-1]
                for m in range(rt.shape[0] - 2, -1, -1):
                    base = jnp.where(kind == m, rates[m], base)
                return base

            cuts = [slice(j * LANES, (j + 1) * LANES) for j in range(tiles)]
            for x in range(nx):
                for j in range(tiles):
                    base = base_of(matv[x : x + 1, cuts[j]], j)
                    BASE[x, :, cuts[j]] = base
                    RATE[x, :, cuts[j]] = base * (0.2 + 0.8 * denv[x : x + 1, cuts[j]])

        def reciprocal(diagonal):
            guess = pl.reciprocal(diagonal, approx=True)
            return guess * (2.0 - diagonal * guess)

        with jax.named_scope("diagonal"):

            def diagonals(x, carry):
                for s in range(subs):
                    rows = pl.ds(s * SUB, SUB)
                    rate = RATE[x, rows, :]
                    total = None
                    for pair in range(half):
                        csum = jnp.concatenate([CF[pair, 5, rows, :]] * tiles, axis=1)
                        inverse = reciprocal(csum + rate)
                        R[pair, x + 1, rows, :] = inverse
                        total = inverse if pair == 0 else total + inverse
                    SUMR[x, rows, :] = total + total
                return carry

            lax.fori_loop(0, nx, diagonals, 0)

        with jax.named_scope("barrier"):
            most = jnp.logical_or(space == 1, space == n_space - 2)

            @pl.when(most)
            def _():
                pl.semaphore_wait(barrier, n_dir + 3)

            @pl.when(jnp.logical_not(most))
            def _():
                pl.semaphore_wait(barrier, n_dir + 2)

        with jax.named_scope("halo0"):
            start(lambda down: halo(0, down))

        start(lambda down: rows_copy(0, down))

        def sum_group(source, target, g, shift):
            def body(x, carry):
                total = source[g * group, x + shift]
                for d in range(1, group):
                    total = total + source[g * group + d, x + shift]
                if g:
                    total = total + target[x]
                target[x] = total
                return carry

            lax.fori_loop(0, nx, body, 0)

        def x_copy(n, k):
            ref = XE.at[block] if n == EARLY else XL.at[block] if n == LATE else XB.at[n, block]
            return pltpu.make_async_remote_copy(
                src_ref=ref,
                dst_ref=ref,
                send_sem=x_send.at[n, k - 1],
                recv_sem=x_recv.at[n, k - 1],
                device_id={"dir": lax.rem(block + k, n_dir)},
                device_id_type=MESH,
            )

        def z_copy(n, aside=False):
            ref = ZE.at[band] if n == EARLY else ZL.at[band] if n == LATE else ZB.at[n, band]
            return pltpu.make_async_remote_copy(
                src_ref=ref,
                dst_ref=ref,
                send_sem=z_send.at[n],
                recv_sem=z_recv.at[n],
                device_id={"dir": before if aside else block, "band": other_band},
                device_id_type=MESH,
            )

        def x_start(n):
            for k in range(1, n_dir):
                x_copy(n, k).start()

        def x_end(n):
            for k in range(1, n_dir):
                x_copy(n, k).wait_recv()
            terms = [
                XE[k] if n == EARLY else XL[k] if n == LATE else XB[n, k] for k in range(n_dir)
            ]
            total = terms[0]
            for term in terms[1:]:
                total = total + term
            return total

        def x_then_z(n):
            total = x_end(n)
            if n == EARLY:
                ZE[band] = total
                z_copy(n).start()
            elif n == LATE:
                ZL[band] = total
                z_copy(n).start()
            else:
                ZB[n, band] = total

                @pl.when(shared)
                def _():
                    z_copy(n, True).start()

                @pl.when(jnp.logical_not(shared))
                def _():
                    z_copy(n).start()

        def exchange_end(n):
            z_copy(n).wait_recv()
            if n == EARLY:
                return ZE[0] + ZE[1]
            if n == LATE:
                return ZL[0] + ZL[1]
            return ZB[n, 0] + ZB[n, 1]

        def exchange_drain(n):
            for k in range(1, n_dir):
                x_copy(n, k).wait_send()
            z_copy(n).wait_send()

        def folded(value):
            return jnp.sum(value, axis=0, keepdims=True)

        with jax.named_scope("sum_a"):
            for g in range(ndir // group):
                loads_a[g].wait()
                sum_group(A, SUMA, g, 0 if g * group < half else 1)
            for x in range(nx):
                XB[0, block, x : x + 1, :] = folded(RATE[x] * SUMA[x])
            x_start(0)
            for x in range(nx):
                XB[THIRD, block, x : x + 1, :] = folded(BASE[x] * wide_weight * SUMR[x])
            x_start(THIRD)
        with jax.named_scope("sum_p"):
            for g in range(ndir // group):
                loads_p[g].wait()
                sum_group(PV, SUMP, g, 0)
            for x in range(nx):
                share = folded(wide_weight * SUMP[x])
                XB[1, block, x : x + 1, :] = share
                TL[x : x + 1, :] = share * mean_scale[:, :1]
                TB[x] = jnp.broadcast_to(TL[x : x + 1, :], (SUB, plane))
            x_start(1)

        for x in range(nx):
            for buffer in (SUMA, SUMP, SUMG):
                buffer[x] = jnp.zeros((nbands, plane), jnp.float32)

        lane8 = lax.broadcasted_iota(jnp.int32, (SUB, LANES), 1)
        low_lanes = lane8 < LANES // 2
        edge_first = lane8 == 0
        edge_last = lane8 == LANES - 1

        def stream(forward_y, up_z, pair, rows, field, near_x):
            cx = CF[pair, 0, rows, :]
            cy = [CF[pair, 1 + i, rows, :] for i in range(3)]
            cz = CF[pair, 4, rows, :]
            turn = [pltpu.roll(v, LANES - 1 if forward_y else 1, 1) for v in field]
            halfway = [pltpu.roll(v, LANES // 2, 1) for v in field]
            values = []
            for j in range(tiles):
                moved = turn[j]
                if forward_y:
                    coef = cy[(0, 1, 2)[j % 3]]
                    if j % 3 != 2:
                        moved = jnp.where(edge_last, turn[j + 1], moved)
                else:
                    coef = cy[(2, 1, 0)[j % 3]]
                    if j % 3 != 0:
                        moved = jnp.where(edge_first, turn[j - 1], moved)
                value = cx * near_x[j] + coef * moved
                if up_z:
                    if j + 2 < tiles:
                        value = value + cz * jnp.where(low_lanes, halfway[j + 1], halfway[j + 2])
                    elif j + 1 < tiles:
                        value = value + cz * jnp.where(low_lanes, halfway[j + 1], 0.0)
                else:
                    if j >= 2:
                        value = value + cz * jnp.where(low_lanes, halfway[j - 2], halfway[j - 1])
                    elif j >= 1:
                        value = value + cz * jnp.where(low_lanes, 0.0, halfway[j - 1])
                values.append(value)
            return values

        def split(ref_rows):
            return [ref_rows[:, c] for c in cuts]

        def join(parts):
            return jnp.concatenate(parts, axis=1)

        def slab_a(forward_y, side, x):
            for s in range(subs):
                rows = pl.ds(s * SUB, SUB)
                total = None
                for pair in range(half):
                    d = pair + side * half
                    own, other = x + side, x + 1 - side
                    near = stream(
                        forward_y, pair % 2 == 0, pair, rows, split(A[d, own, rows, :]), split(A[d, other, rows, :])
                    )
                    value = join(near) * R[pair, x + 1, rows, :]
                    D[d, own, rows, :] = value
                    total = value if pair == 0 else total + value
                SUMA[x, rows, :] = SUMA[x, rows, :] + total

        def slab_b(forward_y, side, x):
            warm = split(TB[x])
            for s in range(subs):
                rows = pl.ds(s * SUB, SUB)
                source = split(WS[x + 2 - 2 * side, rows, :])
                own_source = split(WS[x + 1, rows, :])
                total_g, total_e, total_h = None, None, None
                for pair in range(half):
                    d = pair + side * half
                    own, other = x + side, x + 1 - side
                    beside_a = split(D[d, other, rows, :])
                    beside_r = split(R[pair, x + 2 - 2 * side, rows, :])
                    near_x = [beside_a[j] + source[j] * beside_r[j] for j in range(tiles)]
                    own_a = split(D[d, own, rows, :])
                    inverse = split(R[pair, x + 1, rows, :])
                    field = [own_a[j] + own_source[j] * inverse[j] for j in range(tiles)]
                    near = stream(forward_y, pair % 2 == 0, pair, rows, field, near_x)
                    value = [near[j] * inverse[j] for j in range(tiles)]
                    out[d, x, rows, :] = join(value)
                    excess = split(PV[d, x, rows, :])
                    excess = [excess[j] - warm[j] for j in range(tiles)]
                    both_duals = [field[j] + value[j] for j in range(tiles)]
                    part_g = [both_duals[j] * excess[j] for j in range(tiles)]
                    part_e = [inverse[j] * excess[j] for j in range(tiles)]
                    total_g = part_g if pair == 0 else [total_g[j] + part_g[j] for j in range(tiles)]
                    total_e = part_e if pair == 0 else [total_e[j] + part_e[j] for j in range(tiles)]
                    total_h = both_duals if pair == 0 else [total_h[j] + both_duals[j] for j in range(tiles)]
                SUMG[x, rows, :] = SUMG[x, rows, :] + join(total_g)
                SUMP[x, rows, :] = SUMP[x, rows, :] + join(total_e)
                SUMA[x, rows, :] = SUMA[x, rows, :] + join(total_h)

        def sweep(step, forward_y, hooks):
            def layer(i, carry):
                for at, hook in hooks["before"].items():
                    pl.when(i == at)(hook)
                for side in range(2):
                    x = i if side == 0 else last - i
                    (slab_b if step else slab_a)(forward_y, side, x)
                for at, hook in hooks["after"]:
                    pl.when(i == at)(hook)
                return carry

            lax.fori_loop(0, nx, layer, 0)

        def both(step, hooks):
            @pl.when(ahead)
            def _():
                sweep(step, True, hooks)

            @pl.when(jnp.logical_not(ahead))
            def _():
                sweep(step, False, hooks)

        def set_source(x, slot, row):
            WS[slot] = wide_weight * row

        def wait_halo0():
            with jax.named_scope("waithalo0"):
                arrive(lambda down: halo(0, down))

        def send_halo1():
            start(lambda down: halo(1, down))

        def middle0():
            with jax.named_scope("middle0"):
                x_then_z(0)

        def middle_t():
            with jax.named_scope("middleT"):
                x_then_z(1)
                x_then_z(THIRD)

        with jax.named_scope("sweepA"):
            both(0, {"before": {last: wait_halo0}, "after": ((0, send_halo1), (MIDDLE0, middle0))})
        with jax.named_scope("fold1"):
            for x in range(nx):
                XB[SECOND, block, x : x + 1, :] = folded(BASE[x] * SUMA[x])
                SUMA[x] = jnp.zeros((nbands, plane), jnp.float32)
            x_start(SECOND)

        with jax.named_scope("halodiag"):
            arrive(lambda down: rows_copy(0, down))

            def halo_diagonal(way):
                own = nx + 1 if way == 0 else 0
                for j in range(tiles):
                    base = base_of(HR[way, 1, :, cuts[j]], j)
                    rate = base * (0.2 + 0.8 * HR[way, 0, :, cuts[j]])
                    for pair in range(half):
                        R[pair, own, :, cuts[j]] = reciprocal(CF[pair, 5] + rate)

            @pl.when(has_high)
            def _():
                halo_diagonal(0)

            @pl.when(has_low)
            def _():
                halo_diagonal(1)

        middle_t()
        with jax.named_scope("end0"):
            coupling = exchange_end(0)
        with jax.named_scope("source0"):
            cell_source = NDIR * NB * owv[...]
            first_source = coupling + cell_source
            for x in range(nx):
                SV[x] = first_source[x : x + 1]
            start(lambda down: rows_copy(1, down))
        with jax.named_scope("source1"):
            for x in range(nx):
                source = wide_weight * first_source[x : x + 1]
                WS[x + 1] = source

        def wait_halo1():
            with jax.named_scope("waithalo1"):
                arrive(lambda down: halo(1, down))
                arrive(lambda down: rows_copy(1, down))

                @pl.when(has_high)
                def _():
                    WS[nx + 1] = wide_weight * SH[0]

                @pl.when(jnp.logical_not(has_high))
                def _():
                    WS[nx + 1] = jnp.zeros((nbands, plane), jnp.float32)

                @pl.when(has_low)
                def _():
                    WS[0] = wide_weight * SH[1]

                @pl.when(jnp.logical_not(has_low))
                def _():
                    WS[0] = jnp.zeros((nbands, plane), jnp.float32)

        def middle1():
            with jax.named_scope("middle1"):
                x_then_z(SECOND)

        def gradient_sums(x):
            base = 0.8 * BASE[x]
            shift = SH_T[x : x + 1, :]
            slope = folded(base * (SUMG[x] - shift * SUMA[x]))
            return slope, folded(base * wide_weight * (SUMP[x] - shift * SUMR[x]))

        def send_early():
            with jax.named_scope("early"):
                SH_T[...] = exchange_end(1) - TL[...]
                for row in range(nx - 2):
                    slope, share = gradient_sums(row + 1)
                    XE[block, row : row + 1, :] = slope
                    XE[block, nx - 2 + row : nx - 1 + row, :] = share
                x_start(EARLY)

        with jax.named_scope("sweepB"):
            both(1, {"before": {last: wait_halo1}, "after": ((MIDDLE1 + 1 * odd, middle1), (last - 1, send_early))})
        with jax.named_scope("late"):
            for row, x in ((0, 0), (1, last)):
                slope, share = gradient_sums(x)
                XL[block, row : row + 1, :] = slope
                XL[block, 2 + row : 3 + row, :] = share
            x_start(LATE)
        with jax.named_scope("end1"):
            first_source = SV[:, 0]
            total = exchange_end(SECOND) + first_source * exchange_end(THIRD)
            scale = 0.2 + 0.8 * denv[...]
            second_source = scale * total + NDIR * NB * owv[...]
            for x in range(nx):
                WS[x + 1] = wide_weight * second_source[x : x + 1]
        with jax.named_scope("final"):

            def finish(x, carry):
                source = WS[x + 1]
                for d in range(ndir):
                    out[d, x] = out[d, x] + source * R[d % half, x + 1]
                return carry

            lax.fori_loop(0, nx, finish, 0)
        with jax.named_scope("early_x"):
            x_then_z(EARLY)
        with jax.named_scope("late_x"):
            x_then_z(LATE)
        with jax.named_scope("last_z"):
            inner, outer = exchange_end(EARLY), exchange_end(LATE)
            slope = jnp.concatenate([outer[0:1], inner[: nx - 2], outer[1:2]], axis=0)
            share = jnp.concatenate([outer[2:3], inner[nx - 2 :], outer[3:4]], axis=0)
            grad[...] = (slope + second_source * share) * (-0.125 / ITERS)
        with jax.named_scope("drain"):
            for n in range(6):
                exchange_drain(n)
            for step in range(2):
                drain(lambda down: halo(step, down))
                drain(lambda down: rows_copy(step, down))

    return kernel


def write_out(dual, grad, dual_out, grad_out, sem):
    count = dual.shape[0]
    copies = [pltpu.make_async_copy(grad, grad_out, sem.at[count])]
    for d in range(count):
        copies.append(pltpu.make_async_copy(dual.at[d], dual_out.at[d], sem.at[d]))
    for copy in copies:
        copy.start()
    for copy in copies:
        copy.wait()


def solution(mesh):
    n_space, n_dir, n_band = mesh.shape["space"], mesh.shape["dir"], mesh.shape["band"]
    placed = (
        P("dir", "band", "space", None),
        P("dir", "band", "space", None),
        P("space", None),
        P("space", None),
        P(None, "band"),
        P("band"),
        P(),
        P("space", None),
    )

    def on_device(adj, pri, den, mat, rt, gs, hc, ow):
        ndir, nbands, nx, plane = adj.shape
        half = ndir // 2
        f32 = jnp.float32
        vmem = lambda *shape: pltpu.VMEM(shape, f32)
        dma = pltpu.SemaphoreType.DMA
        call = pl.pallas_call(
            make_kernel(ndir, nbands, nx, plane, n_space, n_dir, n_band),
            out_shape=(
                jax.ShapeDtypeStruct((ndir, nx, nbands, plane), f32),
                jax.ShapeDtypeStruct((nx, plane), f32),
            ),
            in_specs=[pl.BlockSpec(memory_space=pltpu.HBM)] * 8,
            out_specs=(pl.BlockSpec(memory_space=pltpu.VMEM),) * 2,
            scratch_shapes=[
                vmem(ndir, nx + 1, nbands, plane),
                vmem(ndir, nx, nbands, plane),
                vmem(ndir, nx + 1, nbands, plane),
                vmem(half, nx + 2, nbands, plane),
                vmem(nx, nbands, plane),
                vmem(nx, nbands, plane),
                vmem(nx + 2, nbands, plane),
                vmem(half, 6, nbands, LANES),
                vmem(nx, nbands, plane),
                vmem(nx, nbands, plane),
                vmem(nx, nbands, plane),
                vmem(nx, nbands, plane),
                vmem(nx, SUB, plane),
                vmem(nx, 1, plane),
                vmem(2, 1, plane),
                vmem(2, 2, 1, plane),
                vmem(2, 2, 1, plane),
                vmem(nx, plane),
                pltpu.VMEM((nx, plane), jnp.int32),
                vmem(*rt.shape),
                vmem(1, nbands),
                vmem(1, NB),
                vmem(nx, plane),
                vmem(nx, plane),
                vmem(nx, plane),
                vmem(4, n_dir, nx, plane),
                vmem(4, n_band, nx, plane),
                vmem(n_dir, 2 * (nx - 2), plane),
                vmem(n_dir, 4, plane),
                vmem(n_band, 2 * (nx - 2), plane),
                vmem(n_band, 4, plane),
                dma((2, 4)),
                dma((6,)),
                dma((2, 2)),
                dma((2, 2)),
                dma((2, 2)),
                dma((2, 2)),
                dma((6, n_dir - 1)),
                dma((6, n_dir - 1)),
                dma((6,)),
                dma((6,)),
            ],
            compiler_params=pltpu.CompilerParams(
                collective_id=0, has_side_effects=True, vmem_limit_bytes=40 * 1024 * 1024
            ),
        )
        turn = lambda v: jnp.transpose(v, (0, 2, 1, 3))
        operands = (
            turn(adj), turn(pri), den, mat, rt, gs.reshape(1, nbands), hc.reshape(1, NB), ow
        )
        dual, grad = call(*[pltpu.with_memory_space_constraint(v, pltpu.HBM) for v in operands])
        dual, grad = pl.pallas_call(
            write_out,
            out_shape=(
                jax.ShapeDtypeStruct(dual.shape, f32),
                jax.ShapeDtypeStruct(grad.shape, f32),
            ),
            in_specs=[pl.BlockSpec(memory_space=pltpu.VMEM)] * 2,
            out_specs=(pl.BlockSpec(memory_space=pltpu.HBM),) * 2,
            scratch_shapes=[dma((ndir + 1,))],
            compiler_params=pltpu.CompilerParams(vmem_limit_bytes=1024 * 1024),
        )(dual, grad)
        return turn(dual), grad

    return jax.shard_map(
        on_device,
        mesh=mesh,
        in_specs=placed,
        out_specs=(P("dir", "band", "space", None), P("space", None)),
        check_vma=False,
    )
```

```python
import jax
import jax.numpy as jnp
import numpy as np
from jax import lax
from jax.experimental import pallas as pl
from jax.experimental.pallas import tpu as pltpu
from jax.sharding import PartitionSpec as P

NDIR = 64
NB = 32
NY = 192
ITERS = 2
LANES = 128
SUB = 8
SECOND = 2
THIRD = 3
EARLY = 4
LATE = 5
MIDDLE0 = 3
MIDDLE1 = 2
MESH = pl.DeviceIdType.MESH


def direction_constants(half, blocks):
    index = np.arange(blocks * half, dtype=np.float32)
    azimuth = np.float32(np.pi) * (index + np.float32(0.5)) / np.float32(NDIR // 2)
    azimuth = azimuth - np.float32(np.pi / 2)
    pair = np.arange(blocks * half) % half
    along_z = np.float32(0.4) * (1 - 2 * (pair % 2)).astype(np.float32)
    tilt = np.sqrt(np.float32(1.0) - along_z * along_z)
    along_x = np.abs(tilt * np.cos(azimuth))
    along_y = np.abs(tilt * np.sin(azimuth))
    return (
        along_x.reshape(blocks, half),
        along_y.reshape(blocks, half),
        np.abs(along_z).reshape(blocks, half),
    )


def by_block(block, values):
    chosen = jnp.float32(values[-1])
    for index in range(len(values) - 2, -1, -1):
        chosen = jnp.where(block == index, jnp.float32(values[index]), chosen)
    return chosen


def make_kernel(ndir, nbands, nx, plane, n_space, n_dir, n_band):
    half = ndir // 2
    tiles = plane // LANES
    subs = nbands // SUB
    last = nx - 1
    const_x, const_y, const_z = direction_constants(half, n_dir)

    def kernel(
        adj, pri, den, mat, rt, gs, hc, ow,
        out, grad,
        A, PV, D, R, RATE, BASE, WS, CF, SUMA, SUMP, SUMR, SUMG, TB, SV, SH, HS, HR,
        denv, matv, rtv, gsv, hcv, owv, TL, SH_T,
        XB, ZB, XE, XL, ZE, ZL,
        load_sem, small_sem, h_send, h_recv, r_send, r_recv, x_send, x_recv, z_send, z_recv,
    ):
        space = lax.axis_index("space")
        block = lax.axis_index("dir")
        band = lax.axis_index("band")
        other_band = 1 - band
        odd = lax.rem(space, 2)
        has_low = space > 0
        has_high = space < n_space - 1

        barrier = pltpu.get_barrier_semaphore()
        for k in range(1, n_dir):
            peer = lax.rem(block + k, n_dir)
            pl.semaphore_signal(barrier, inc=1, device_id={"dir": peer}, device_id_type=MESH)
        before, after = lax.rem(block + n_dir - 1, n_dir), lax.rem(block + 1, n_dir)
        pl.semaphore_signal(barrier, inc=1, device_id={"band": other_band}, device_id_type=MESH)
        shared = jnp.logical_or(space < 2, space >= n_space - 2)

        @pl.when(shared)
        def _():
            pl.semaphore_signal(
                barrier, inc=1, device_id={"dir": after, "band": other_band}, device_id_type=MESH
            )

        @pl.when(has_low)
        def _():
            pl.semaphore_signal(barrier, inc=1, device_id={"space": space - 1}, device_id_type=MESH)

        @pl.when(has_high)
        def _():
            pl.semaphore_signal(barrier, inc=1, device_id={"space": space + 1}, device_id_type=MESH)

        smalls = [
            pltpu.make_async_copy(src, dst, small_sem.at[i])
            for i, (src, dst) in enumerate(
                ((den, denv), (mat, matv), (rt, rtv), (gs, gsv), (hc, hcv), (ow, owv))
            )
        ]
        group = 4
        loads_a = []
        loads_p = []
        for g in range(ndir // group):
            first = g * group
            shift = 0 if first < half else 1
            loads_a.append(
                pltpu.make_async_copy(
                    adj.at[pl.ds(first, group)],
                    A.at[pl.ds(first, group), pl.ds(shift, nx)],
                    load_sem.at[0, g],
                )
            )
            loads_p.append(
                pltpu.make_async_copy(
                    pri.at[pl.ds(first, group)], PV.at[pl.ds(first, group)], load_sem.at[1, g]
                )
            )
        for copy in smalls:
            copy.start()

        def beside(src, dst, down, send_sem, recv_sem):
            return pltpu.make_async_remote_copy(
                src_ref=src,
                dst_ref=dst,
                send_sem=send_sem,
                recv_sem=recv_sem,
                device_id={"space": space - 1 if down else space + 1},
                device_id_type=MESH,
            )

        def halo(step, down):
            way = 0 if down else 1
            rows = pl.ds(0 if down else half, half)
            buffer = D if step else A
            if step:
                src = D.at[rows, 0 if down else nx]
            else:
                src = adj.at[rows, 0 if down else last]
            dst = buffer.at[rows, nx if down else 0]
            return beside(src, dst, down, h_send.at[step, way], h_recv.at[step, way])

        def rows_copy(step, down):
            way = 0 if down else 1
            if step == 0:
                src, dst = HS.at[way], HR.at[way]
            else:
                src, dst = SV.at[0 if down else last], SH.at[way]
            return beside(src, dst, down, r_send.at[step, way], r_recv.at[step, way])

        def both_ways(make, act, receive=False):
            @pl.when(has_high if receive else has_low)
            def _():
                act(make(True))

            @pl.when(has_low if receive else has_high)
            def _():
                act(make(False))

        def start_far(make):
            @pl.when(jnp.logical_and(has_high, odd == 1))
            def _():
                make(False).start()

            @pl.when(jnp.logical_and(has_low, odd == 0))
            def _():
                make(True).start()

        def start_near(make):
            @pl.when(odd == 1)
            def _():
                make(True).start()

            @pl.when(odd == 0)
            def _():
                make(False).start()

        def start(make):
            start_far(make)
            start_near(make)

        def arrive(make):
            both_ways(make, lambda copy: copy.wait_recv(), receive=True)

        def drain(make):
            both_ways(make, lambda copy: copy.wait_send())

        @pl.when(jnp.logical_not(has_high))
        def _():
            def clear(d, carry):
                for buffer in (A, D):
                    buffer[d, nx] = jnp.zeros((nbands, plane), jnp.float32)
                R[d, nx + 1] = jnp.zeros((nbands, plane), jnp.float32)
                return carry

            lax.fori_loop(0, half, clear, 0)

        @pl.when(jnp.logical_not(has_low))
        def _():
            def clear(d, carry):
                for buffer in (A, D):
                    buffer[half + d, 0] = jnp.zeros((nbands, plane), jnp.float32)
                R[d, 0] = jnp.zeros((nbands, plane), jnp.float32)
                return carry

            lax.fori_loop(0, half, clear, 0)

        with jax.named_scope("smallwait"):
            for copy in smalls:
                copy.wait()
            for copy in loads_a:
                copy.start()
            for copy in loads_p:
                copy.start()
        with jax.named_scope("tables"):
            for way, x in ((0, 0), (1, last)):
                HS[way, 0] = denv[x : x + 1, :]
                HS[way, 1] = matv[x : x + 1, :].astype(jnp.float32)
            row_index = lax.broadcasted_iota(jnp.int32, (nbands, nbands), 0)
            lane_index = lax.broadcasted_iota(jnp.int32, (nbands, nbands), 1)

            def column(row):
                spread = jnp.where(row_index == lane_index, row, 0.0)
                return jnp.broadcast_to(jnp.sum(spread, axis=1, keepdims=True), (nbands, LANES))

            rates = [column(rtv[m : m + 1, :]) for m in range(rt.shape[0])]
            speed = column(gsv[...])
            heat = hcv[...]
            total_heat = jnp.sum(heat, axis=1, keepdims=True)
            wide_row = lax.broadcasted_iota(jnp.int32, (nbands, NB), 0) + band * nbands
            wide_lane = lax.broadcasted_iota(jnp.int32, (nbands, NB), 1)
            local_heat = jnp.sum(jnp.where(wide_row == wide_lane, heat, 0.0), axis=1, keepdims=True)
            weight = jnp.broadcast_to(local_heat / (NDIR * total_heat), (nbands, LANES))
            wide_weight = jnp.concatenate([weight] * tiles, axis=1)
            mean_scale = 1.0 / (ndir * jnp.sum(weight, axis=0, keepdims=True))
            lane = lax.broadcasted_iota(jnp.int32, (nbands, LANES), 1)
            ahead = block >= n_dir // 2
            middle = jnp.where(ahead, 63, 64)
            edge = jnp.where(ahead, LANES - 1, 0)
            for pair in range(half):
                sx = speed * by_block(block, const_x[:, pair])
                sy = speed * by_block(block, const_y[:, pair])
                sz = speed * jnp.float32(const_z[0, pair])
                CF[pair, 0] = sx
                CF[pair, 1] = sy
                CF[pair, 2] = jnp.where(lane == middle, 0.0, sy)
                CF[pair, 3] = jnp.where(lane == edge, 0.0, sy)
                CF[pair, 4] = sz
                CF[pair, 5] = sx + sy + sz

            def base_of(kind_row, j):
                kind = jnp.broadcast_to(kind_row, (nbands, LANES))
                base = rates[-1]
                for m in range(rt.shape[0] - 2, -1, -1):
                    base = jnp.where(kind == m, rates[m], base)
                return base

            cuts = [slice(j * LANES, (j + 1) * LANES) for j in range(tiles)]
            for x in range(nx):
                for j in range(tiles):
                    base = base_of(matv[x : x + 1, cuts[j]], j)
                    BASE[x, :, cuts[j]] = base
                    RATE[x, :, cuts[j]] = base * (0.2 + 0.8 * denv[x : x + 1, cuts[j]])

        def reciprocal(diagonal):
            guess = pl.reciprocal(diagonal, approx=True)
            return guess * (2.0 - diagonal * guess)

        with jax.named_scope("diagonal"):

            def diagonals(x, carry):
                for s in range(subs):
                    rows = pl.ds(s * SUB, SUB)
                    rate = RATE[x, rows, :]
                    total = None
                    for pair in range(half):
                        csum = jnp.concatenate([CF[pair, 5, rows, :]] * tiles, axis=1)
                        inverse = reciprocal(csum + rate)
                        R[pair, x + 1, rows, :] = inverse
                        total = inverse if pair == 0 else total + inverse
                    SUMR[x, rows, :] = total + total
                return carry

            lax.fori_loop(0, nx, diagonals, 0)

        with jax.named_scope("barrier"):
            most = jnp.logical_or(space == 1, space == n_space - 2)

            @pl.when(most)
            def _():
                pl.semaphore_wait(barrier, n_dir + 3)

            @pl.when(jnp.logical_not(most))
            def _():
                pl.semaphore_wait(barrier, n_dir + 2)

        with jax.named_scope("halo0"):
            start_far(lambda down: halo(0, down))

        start(lambda down: rows_copy(0, down))

        def sum_group(source, target, g, shift):
            def body(x, carry):
                total = source[g * group, x + shift]
                for d in range(1, group):
                    total = total + source[g * group + d, x + shift]
                if g:
                    total = total + target[x]
                target[x] = total
                return carry

            lax.fori_loop(0, nx, body, 0)

        def x_copy(n, k):
            ref = XE.at[block] if n == EARLY else XL.at[block] if n == LATE else XB.at[n, block]
            return pltpu.make_async_remote_copy(
                src_ref=ref,
                dst_ref=ref,
                send_sem=x_send.at[n, k - 1],
                recv_sem=x_recv.at[n, k - 1],
                device_id={"dir": lax.rem(block + k, n_dir)},
                device_id_type=MESH,
            )

        def z_copy(n, aside=False):
            ref = ZE.at[band] if n == EARLY else ZL.at[band] if n == LATE else ZB.at[n, band]
            return pltpu.make_async_remote_copy(
                src_ref=ref,
                dst_ref=ref,
                send_sem=z_send.at[n],
                recv_sem=z_recv.at[n],
                device_id={"dir": before if aside else block, "band": other_band},
                device_id_type=MESH,
            )

        def x_start(n):
            for k in range(1, n_dir):
                x_copy(n, k).start()

        def x_end(n):
            for k in range(1, n_dir):
                x_copy(n, k).wait_recv()
            terms = [
                XE[k] if n == EARLY else XL[k] if n == LATE else XB[n, k] for k in range(n_dir)
            ]
            total = terms[0]
            for term in terms[1:]:
                total = total + term
            return total

        def x_then_z(n):
            total = x_end(n)
            if n == EARLY:
                ZE[band] = total
                z_copy(n).start()
            elif n == LATE:
                ZL[band] = total
                z_copy(n).start()
            else:
                ZB[n, band] = total

                @pl.when(shared)
                def _():
                    z_copy(n, True).start()

                @pl.when(jnp.logical_not(shared))
                def _():
                    z_copy(n).start()

        def exchange_end(n):
            z_copy(n).wait_recv()
            if n == EARLY:
                return ZE[0] + ZE[1]
            if n == LATE:
                return ZL[0] + ZL[1]
            return ZB[n, 0] + ZB[n, 1]

        def exchange_drain(n):
            for k in range(1, n_dir):
                x_copy(n, k).wait_send()
            z_copy(n).wait_send()

        def folded(value):
            return jnp.sum(value, axis=0, keepdims=True)

        with jax.named_scope("sum_a"):
            for g in range(ndir // group):
                loads_a[g].wait()
                sum_group(A, SUMA, g, 0 if g * group < half else 1)
            for x in range(nx):
                XB[0, block, x : x + 1, :] = folded(RATE[x] * SUMA[x])
            x_start(0)
            for x in range(nx):
                XB[THIRD, block, x : x + 1, :] = folded(BASE[x] * wide_weight * SUMR[x])
        with jax.named_scope("sum_p"):
            for g in range(ndir // group):
                loads_p[g].wait()
                sum_group(PV, SUMP, g, 0)
            for x in range(nx):
                share = folded(wide_weight * SUMP[x])
                XB[1, block, x : x + 1, :] = share
                TL[x : x + 1, :] = share * mean_scale[:, :1]
                TB[x] = jnp.broadcast_to(TL[x : x + 1, :], (SUB, plane))
            x_start(1)

        for x in range(nx):
            for buffer in (SUMA, SUMP, SUMG):
                buffer[x] = jnp.zeros((nbands, plane), jnp.float32)

        lane8 = lax.broadcasted_iota(jnp.int32, (SUB, LANES), 1)
        low_lanes = lane8 < LANES // 2
        edge_first = lane8 == 0
        edge_last = lane8 == LANES - 1

        def stream(forward_y, up_z, pair, rows, field, near_x):
            cx = CF[pair, 0, rows, :]
            cy = [CF[pair, 1 + i, rows, :] for i in range(3)]
            cz = CF[pair, 4, rows, :]
            turn = [pltpu.roll(v, LANES - 1 if forward_y else 1, 1) for v in field]
            halfway = [pltpu.roll(v, LANES // 2, 1) for v in field]
            values = []
            for j in range(tiles):
                moved = turn[j]
                if forward_y:
                    coef = cy[(0, 1, 2)[j % 3]]
                    if j % 3 != 2:
                        moved = jnp.where(edge_last, turn[j + 1], moved)
                else:
                    coef = cy[(2, 1, 0)[j % 3]]
                    if j % 3 != 0:
                        moved = jnp.where(edge_first, turn[j - 1], moved)
                value = cx * near_x[j] + coef * moved
                if up_z:
                    if j + 2 < tiles:
                        value = value + cz * jnp.where(low_lanes, halfway[j + 1], halfway[j + 2])
                    elif j + 1 < tiles:
                        value = value + cz * jnp.where(low_lanes, halfway[j + 1], 0.0)
                else:
                    if j >= 2:
                        value = value + cz * jnp.where(low_lanes, halfway[j - 2], halfway[j - 1])
                    elif j >= 1:
                        value = value + cz * jnp.where(low_lanes, 0.0, halfway[j - 1])
                values.append(value)
            return values

        def split(ref_rows):
            return [ref_rows[:, c] for c in cuts]

        def join(parts):
            return jnp.concatenate(parts, axis=1)

        def slab_a(forward_y, side, x):
            for s in range(subs):
                rows = pl.ds(s * SUB, SUB)
                total = None
                for pair in range(half):
                    d = pair + side * half
                    own, other = x + side, x + 1 - side
                    near = stream(
                        forward_y, pair % 2 == 0, pair, rows, split(A[d, own, rows, :]), split(A[d, other, rows, :])
                    )
                    value = join(near) * R[pair, x + 1, rows, :]
                    D[d, own, rows, :] = value
                    total = value if pair == 0 else total + value
                SUMA[x, rows, :] = SUMA[x, rows, :] + total

        def slab_b(forward_y, side, x):
            warm = split(TB[x])
            for s in range(subs):
                rows = pl.ds(s * SUB, SUB)
                source = split(WS[x + 2 - 2 * side, rows, :])
                own_source = split(WS[x + 1, rows, :])
                total_g, total_e, total_h = None, None, None
                for pair in range(half):
                    d = pair + side * half
                    own, other = x + side, x + 1 - side
                    beside_a = split(D[d, other, rows, :])
                    beside_r = split(R[pair, x + 2 - 2 * side, rows, :])
                    near_x = [beside_a[j] + source[j] * beside_r[j] for j in range(tiles)]
                    own_a = split(D[d, own, rows, :])
                    inverse = split(R[pair, x + 1, rows, :])
                    field = [own_a[j] + own_source[j] * inverse[j] for j in range(tiles)]
                    near = stream(forward_y, pair % 2 == 0, pair, rows, field, near_x)
                    value = [near[j] * inverse[j] for j in range(tiles)]
                    out[d, x, rows, :] = join(value)
                    excess = split(PV[d, x, rows, :])
                    excess = [excess[j] - warm[j] for j in range(tiles)]
                    both_duals = [field[j] + value[j] for j in range(tiles)]
                    part_g = [both_duals[j] * excess[j] for j in range(tiles)]
                    part_e = [inverse[j] * excess[j] for j in range(tiles)]
                    total_g = part_g if pair == 0 else [total_g[j] + part_g[j] for j in range(tiles)]
                    total_e = part_e if pair == 0 else [total_e[j] + part_e[j] for j in range(tiles)]
                    total_h = both_duals if pair == 0 else [total_h[j] + both_duals[j] for j in range(tiles)]
                SUMG[x, rows, :] = SUMG[x, rows, :] + join(total_g)
                SUMP[x, rows, :] = SUMP[x, rows, :] + join(total_e)
                SUMA[x, rows, :] = SUMA[x, rows, :] + join(total_h)

        def sweep(step, forward_y, hooks):
            def layer(i, carry):
                for side in range(2):
                    pl.when(i == last)(hooks["halo"][side])
                    x = i if side == 0 else last - i
                    (slab_b if step else slab_a)(forward_y, side, x)
                for at, hook in hooks["after"]:
                    pl.when(i == at)(hook)
                return carry

            lax.fori_loop(0, nx, layer, 0)

        def both(step, hooks):
            @pl.when(ahead)
            def _():
                sweep(step, True, hooks)

            @pl.when(jnp.logical_not(ahead))
            def _():
                sweep(step, False, hooks)

        def set_source(x, slot, row):
            WS[slot] = wide_weight * row

        def wait_halo0(side):
            def hook():
                @pl.when(has_low if side else has_high)
                def _():
                    halo(0, side == 0).wait_recv()

            return hook

        def send_halo1():
            start_far(lambda down: halo(1, down))

        def send_near0():
            start_near(lambda down: halo(0, down))

        def middle0():
            with jax.named_scope("middle0"):
                x_then_z(0)
                x_start(THIRD)

        def middle_t():
            with jax.named_scope("middleT"):
                x_then_z(1)

        with jax.named_scope("sweepA"):
            both(0, {"halo": [wait_halo0(0), wait_halo0(1)], "after": ((1, send_near0), (0, send_halo1), (MIDDLE0, middle0))})
        with jax.named_scope("fold1"):
            for x in range(nx):
                XB[SECOND, block, x : x + 1, :] = folded(BASE[x] * SUMA[x])
                SUMA[x] = jnp.zeros((nbands, plane), jnp.float32)
            x_start(SECOND)

        with jax.named_scope("halodiag"):
            arrive(lambda down: rows_copy(0, down))

            def halo_diagonal(way):
                own = nx + 1 if way == 0 else 0
                for j in range(tiles):
                    base = base_of(HR[way, 1, :, cuts[j]], j)
                    rate = base * (0.2 + 0.8 * HR[way, 0, :, cuts[j]])
                    for pair in range(half):
                        R[pair, own, :, cuts[j]] = reciprocal(CF[pair, 5] + rate)

            @pl.when(has_high)
            def _():
                halo_diagonal(0)

            @pl.when(has_low)
            def _():
                halo_diagonal(1)

        middle_t()
        with jax.named_scope("end0"):
            coupling = exchange_end(0)
        start_near(lambda down: halo(1, down))
        with jax.named_scope("source0"):
            cell_source = NDIR * NB * owv[...]
            first_source = coupling + cell_source
            for x in range(nx):
                SV[x] = first_source[x : x + 1]
            start(lambda down: rows_copy(1, down))
        with jax.named_scope("source1"):
            for x in range(nx):
                source = wide_weight * first_source[x : x + 1]
                WS[x + 1] = source

        def wait_halo1(side):
            layer, row = (0, 1) if side else (nx + 1, 0)

            def hook():
                with jax.named_scope("waithalo1"):
                    @pl.when(has_low if side else has_high)
                    def _():
                        halo(1, side == 0).wait_recv()
                        rows_copy(1, side == 0).wait_recv()
                        WS[layer] = wide_weight * SH[row]

                    @pl.when(jnp.logical_not(has_low if side else has_high))
                    def _():
                        WS[layer] = jnp.zeros((nbands, plane), jnp.float32)

            return hook

        def middle1():
            with jax.named_scope("middle1"):
                x_then_z(SECOND)
                x_then_z(THIRD)

        def gradient_sums(x):
            base = 0.8 * BASE[x]
            shift = SH_T[x : x + 1, :]
            slope = folded(base * (SUMG[x] - shift * SUMA[x]))
            return slope, folded(base * wide_weight * (SUMP[x] - shift * SUMR[x]))

        def send_early():
            with jax.named_scope("early"):
                SH_T[...] = exchange_end(1) - TL[...]
                for row in range(nx - 2):
                    slope, share = gradient_sums(row + 1)
                    XE[block, row : row + 1, :] = slope
                    XE[block, nx - 2 + row : nx - 1 + row, :] = share
                x_start(EARLY)

        with jax.named_scope("sweepB"):
            both(1, {"halo": [wait_halo1(0), wait_halo1(1)], "after": ((last - 1, middle1), (last - 1, send_early))})
        with jax.named_scope("late"):
            for row, x in ((0, 0), (1, last)):
                slope, share = gradient_sums(x)
                XL[block, row : row + 1, :] = slope
                XL[block, 2 + row : 3 + row, :] = share
            x_start(LATE)
        with jax.named_scope("early_x"):
            x_then_z(EARLY)
        with jax.named_scope("late_x"):
            x_then_z(LATE)
        with jax.named_scope("end1"):
            first_source = SV[:, 0]
            total = exchange_end(SECOND) + first_source * exchange_end(THIRD)
            scale = 0.2 + 0.8 * denv[...]
            second_source = scale * total + NDIR * NB * owv[...]
            for x in range(nx):
                WS[x + 1] = wide_weight * second_source[x : x + 1]
        with jax.named_scope("final"):

            def finish(x, carry):
                source = WS[x + 1]
                for d in range(ndir):
                    out[d, x] = out[d, x] + source * R[d % half, x + 1]
                return carry

            lax.fori_loop(0, nx, finish, 0)
        with jax.named_scope("last_z"):
            inner, outer = exchange_end(EARLY), exchange_end(LATE)
            slope = jnp.concatenate([outer[0:1], inner[: nx - 2], outer[1:2]], axis=0)
            share = jnp.concatenate([outer[2:3], inner[nx - 2 :], outer[3:4]], axis=0)
            grad[...] = (slope + second_source * share) * (-0.125 / ITERS)
        with jax.named_scope("drain"):
            for n in range(6):
                exchange_drain(n)
            for step in range(2):
                drain(lambda down: halo(step, down))
                drain(lambda down: rows_copy(step, down))

    return kernel


def write_out(dual, grad, dual_out, grad_out, sem):
    count = dual.shape[0]
    copies = [pltpu.make_async_copy(grad, grad_out, sem.at[count])]
    for d in range(count):
        copies.append(pltpu.make_async_copy(dual.at[d], dual_out.at[d], sem.at[d]))
    for copy in copies:
        copy.start()
    for copy in copies:
        copy.wait()


def solution(mesh):
    n_space, n_dir, n_band = mesh.shape["space"], mesh.shape["dir"], mesh.shape["band"]
    placed = (
        P("dir", "band", "space", None),
        P("dir", "band", "space", None),
        P("space", None),
        P("space", None),
        P(None, "band"),
        P("band"),
        P(),
        P("space", None),
    )

    def on_device(adj, pri, den, mat, rt, gs, hc, ow):
        ndir, nbands, nx, plane = adj.shape
        half = ndir // 2
        f32 = jnp.float32
        vmem = lambda *shape: pltpu.VMEM(shape, f32)
        dma = pltpu.SemaphoreType.DMA
        call = pl.pallas_call(
            make_kernel(ndir, nbands, nx, plane, n_space, n_dir, n_band),
            out_shape=(
                jax.ShapeDtypeStruct((ndir, nx, nbands, plane), f32),
                jax.ShapeDtypeStruct((nx, plane), f32),
            ),
            in_specs=[pl.BlockSpec(memory_space=pltpu.HBM)] * 8,
            out_specs=(pl.BlockSpec(memory_space=pltpu.VMEM),) * 2,
            scratch_shapes=[
                vmem(ndir, nx + 1, nbands, plane),
                vmem(ndir, nx, nbands, plane),
                vmem(ndir, nx + 1, nbands, plane),
                vmem(half, nx + 2, nbands, plane),
                vmem(nx, nbands, plane),
                vmem(nx, nbands, plane),
                vmem(nx + 2, nbands, plane),
                vmem(half, 6, nbands, LANES),
                vmem(nx, nbands, plane),
                vmem(nx, nbands, plane),
                vmem(nx, nbands, plane),
                vmem(nx, nbands, plane),
                vmem(nx, SUB, plane),
                vmem(nx, 1, plane),
                vmem(2, 1, plane),
                vmem(2, 2, 1, plane),
                vmem(2, 2, 1, plane),
                vmem(nx, plane),
                pltpu.VMEM((nx, plane), jnp.int32),
                vmem(*rt.shape),
                vmem(1, nbands),
                vmem(1, NB),
                vmem(nx, plane),
                vmem(nx, plane),
                vmem(nx, plane),
                vmem(4, n_dir, nx, plane),
                vmem(4, n_band, nx, plane),
                vmem(n_dir, 2 * (nx - 2), plane),
                vmem(n_dir, 4, plane),
                vmem(n_band, 2 * (nx - 2), plane),
                vmem(n_band, 4, plane),
                dma((2, 4)),
                dma((6,)),
                dma((2, 2)),
                dma((2, 2)),
                dma((2, 2)),
                dma((2, 2)),
                dma((6, n_dir - 1)),
                dma((6, n_dir - 1)),
                dma((6,)),
                dma((6,)),
            ],
            compiler_params=pltpu.CompilerParams(
                collective_id=0, has_side_effects=True, vmem_limit_bytes=40 * 1024 * 1024
            ),
        )
        turn = lambda v: jnp.transpose(v, (0, 2, 1, 3))
        operands = (
            turn(adj), turn(pri), den, mat, rt, gs.reshape(1, nbands), hc.reshape(1, NB), ow
        )
        dual, grad = call(*[pltpu.with_memory_space_constraint(v, pltpu.HBM) for v in operands])
        dual, grad = pl.pallas_call(
            write_out,
            out_shape=(
                jax.ShapeDtypeStruct(dual.shape, f32),
                jax.ShapeDtypeStruct(grad.shape, f32),
            ),
            in_specs=[pl.BlockSpec(memory_space=pltpu.VMEM)] * 2,
            out_specs=(pl.BlockSpec(memory_space=pltpu.HBM),) * 2,
            scratch_shapes=[dma((ndir + 1,))],
            compiler_params=pltpu.CompilerParams(vmem_limit_bytes=1024 * 1024),
        )(dual, grad)
        return turn(dual), grad

    return jax.shard_map(
        on_device,
        mesh=mesh,
        in_specs=placed,
        out_specs=(P("dir", "band", "space", None), P("space", None)),
        check_vma=False,
    )
```

```python
import jax
import jax.numpy as jnp
import numpy as np
from jax import lax
from jax.experimental import pallas as pl
from jax.experimental.pallas import tpu as pltpu
from jax.sharding import PartitionSpec as P

NDIR = 64
NB = 32
NY = 192
ITERS = 2
LANES = 128
SUB = 8
SECOND = 2
THIRD = 3
EARLY = 4
LATE = 5
MIDDLE0 = 3
MIDDLE1 = 2
MESH = pl.DeviceIdType.MESH


def direction_constants(half, blocks):
    index = np.arange(blocks * half, dtype=np.float32)
    azimuth = np.float32(np.pi) * (index + np.float32(0.5)) / np.float32(NDIR // 2)
    azimuth = azimuth - np.float32(np.pi / 2)
    pair = np.arange(blocks * half) % half
    along_z = np.float32(0.4) * (1 - 2 * (pair % 2)).astype(np.float32)
    tilt = np.sqrt(np.float32(1.0) - along_z * along_z)
    along_x = np.abs(tilt * np.cos(azimuth))
    along_y = np.abs(tilt * np.sin(azimuth))
    return (
        along_x.reshape(blocks, half),
        along_y.reshape(blocks, half),
        np.abs(along_z).reshape(blocks, half),
    )


def by_block(block, values):
    chosen = jnp.float32(values[-1])
    for index in range(len(values) - 2, -1, -1):
        chosen = jnp.where(block == index, jnp.float32(values[index]), chosen)
    return chosen


def make_kernel(ndir, nbands, nx, plane, n_space, n_dir, n_band):
    half = ndir // 2
    tiles = plane // LANES
    subs = nbands // SUB
    last = nx - 1
    const_x, const_y, const_z = direction_constants(half, n_dir)

    def kernel(
        adj, pri, den, mat, rt, gs, hc, ow,
        out, grad,
        A, PV, D, R, RATE, BASE, WS, CF, SUMA, SUMP, SUMR, SUMG, TB, SV, SH, HS, HR,
        denv, matv, rtv, gsv, hcv, owv, TL, SH_T,
        XB, ZB, XE, XL, ZE, ZL,
        load_sem, small_sem, h_send, h_recv, r_send, r_recv, x_send, x_recv, z_send, z_recv,
    ):
        space = lax.axis_index("space")
        block = lax.axis_index("dir")
        band = lax.axis_index("band")
        other_band = 1 - band
        odd = lax.rem(space, 2)
        has_low = space > 0
        has_high = space < n_space - 1

        barrier = pltpu.get_barrier_semaphore()
        for k in range(1, n_dir):
            peer = lax.rem(block + k, n_dir)
            pl.semaphore_signal(barrier, inc=1, device_id={"dir": peer}, device_id_type=MESH)
        before, after = lax.rem(block + n_dir - 1, n_dir), lax.rem(block + 1, n_dir)
        pl.semaphore_signal(barrier, inc=1, device_id={"band": other_band}, device_id_type=MESH)
        shared = jnp.logical_or(space < 2, space >= n_space - 2)

        @pl.when(shared)
        def _():
            pl.semaphore_signal(
                barrier, inc=1, device_id={"dir": after, "band": other_band}, device_id_type=MESH
            )

        @pl.when(has_low)
        def _():
            pl.semaphore_signal(barrier, inc=1, device_id={"space": space - 1}, device_id_type=MESH)

        @pl.when(has_high)
        def _():
            pl.semaphore_signal(barrier, inc=1, device_id={"space": space + 1}, device_id_type=MESH)

        smalls = [
            pltpu.make_async_copy(src, dst, small_sem.at[i])
            for i, (src, dst) in enumerate(
                ((den, denv), (mat, matv), (rt, rtv), (gs, gsv), (hc, hcv), (ow, owv))
            )
        ]
        group = 4
        loads_a = []
        loads_p = []
        for g in range(ndir // group):
            first = g * group
            shift = 0 if first < half else 1
            loads_a.append(
                pltpu.make_async_copy(
                    adj.at[pl.ds(first, group)],
                    A.at[pl.ds(first, group), pl.ds(shift, nx)],
                    load_sem.at[0, g],
                )
            )
            loads_p.append(
                pltpu.make_async_copy(
                    pri.at[pl.ds(first, group)], PV.at[pl.ds(first, group)], load_sem.at[1, g]
                )
            )
        for copy in smalls:
            copy.start()

        def beside(src, dst, down, send_sem, recv_sem):
            return pltpu.make_async_remote_copy(
                src_ref=src,
                dst_ref=dst,
                send_sem=send_sem,
                recv_sem=recv_sem,
                device_id={"space": space - 1 if down else space + 1},
                device_id_type=MESH,
            )

        def halo(step, down):
            way = 0 if down else 1
            rows = pl.ds(0 if down else half, half)
            buffer = D if step else A
            if step:
                src = D.at[rows, 0 if down else nx]
            else:
                src = adj.at[rows, 0 if down else last]
            dst = buffer.at[rows, nx if down else 0]
            return beside(src, dst, down, h_send.at[step, way], h_recv.at[step, way])

        def rows_copy(step, down):
            way = 0 if down else 1
            if step == 0:
                src, dst = HS.at[way], HR.at[way]
            else:
                src, dst = SV.at[0 if down else last], SH.at[way]
            return beside(src, dst, down, r_send.at[step, way], r_recv.at[step, way])

        def both_ways(make, act, receive=False):
            @pl.when(has_high if receive else has_low)
            def _():
                act(make(True))

            @pl.when(has_low if receive else has_high)
            def _():
                act(make(False))

        def start_far(make):
            @pl.when(jnp.logical_and(has_high, odd == 1))
            def _():
                make(False).start()

            @pl.when(jnp.logical_and(has_low, odd == 0))
            def _():
                make(True).start()

        def start_near(make):
            @pl.when(odd == 1)
            def _():
                make(True).start()

            @pl.when(odd == 0)
            def _():
                make(False).start()

        def start(make):
            start_far(make)
            start_near(make)

        def arrive(make):
            both_ways(make, lambda copy: copy.wait_recv(), receive=True)

        def drain(make):
            both_ways(make, lambda copy: copy.wait_send())

        @pl.when(jnp.logical_not(has_high))
        def _():
            def clear(d, carry):
                for buffer in (A, D):
                    buffer[d, nx] = jnp.zeros((nbands, plane), jnp.float32)
                R[d, nx + 1] = jnp.zeros((nbands, plane), jnp.float32)
                return carry

            lax.fori_loop(0, half, clear, 0)

        @pl.when(jnp.logical_not(has_low))
        def _():
            def clear(d, carry):
                for buffer in (A, D):
                    buffer[half + d, 0] = jnp.zeros((nbands, plane), jnp.float32)
                R[d, 0] = jnp.zeros((nbands, plane), jnp.float32)
                return carry

            lax.fori_loop(0, half, clear, 0)

        with jax.named_scope("smallwait"):
            for copy in smalls:
                copy.wait()
            for copy in loads_a:
                copy.start()
            for copy in loads_p:
                copy.start()
        with jax.named_scope("tables"):
            for way, x in ((0, 0), (1, last)):
                HS[way, 0] = denv[x : x + 1, :]
                HS[way, 1] = matv[x : x + 1, :].astype(jnp.float32)
            row_index = lax.broadcasted_iota(jnp.int32, (nbands, nbands), 0)
            lane_index = lax.broadcasted_iota(jnp.int32, (nbands, nbands), 1)

            def column(row):
                spread = jnp.where(row_index == lane_index, row, 0.0)
                return jnp.broadcast_to(jnp.sum(spread, axis=1, keepdims=True), (nbands, LANES))

            rates = [column(rtv[m : m + 1, :]) for m in range(rt.shape[0])]
            speed = column(gsv[...])
            heat = hcv[...]
            total_heat = jnp.sum(heat, axis=1, keepdims=True)
            wide_row = lax.broadcasted_iota(jnp.int32, (nbands, NB), 0) + band * nbands
            wide_lane = lax.broadcasted_iota(jnp.int32, (nbands, NB), 1)
            local_heat = jnp.sum(jnp.where(wide_row == wide_lane, heat, 0.0), axis=1, keepdims=True)
            weight = jnp.broadcast_to(local_heat / (NDIR * total_heat), (nbands, LANES))
            wide_weight = jnp.concatenate([weight] * tiles, axis=1)
            mean_scale = 1.0 / (ndir * jnp.sum(weight, axis=0, keepdims=True))
            lane = lax.broadcasted_iota(jnp.int32, (nbands, LANES), 1)
            ahead = block >= n_dir // 2
            middle = jnp.where(ahead, 63, 64)
            edge = jnp.where(ahead, LANES - 1, 0)
            for pair in range(half):
                sx = speed * by_block(block, const_x[:, pair])
                sy = speed * by_block(block, const_y[:, pair])
                sz = speed * jnp.float32(const_z[0, pair])
                CF[pair, 0] = sx
                CF[pair, 1] = sy
                CF[pair, 2] = jnp.where(lane == middle, 0.0, sy)
                CF[pair, 3] = jnp.where(lane == edge, 0.0, sy)
                CF[pair, 4] = sz
                CF[pair, 5] = sx + sy + sz

            def base_of(kind_row, j):
                kind = jnp.broadcast_to(kind_row, (nbands, LANES))
                base = rates[-1]
                for m in range(rt.shape[0] - 2, -1, -1):
                    base = jnp.where(kind == m, rates[m], base)
                return base

            cuts = [slice(j * LANES, (j + 1) * LANES) for j in range(tiles)]
            for x in range(nx):
                for j in range(tiles):
                    base = base_of(matv[x : x + 1, cuts[j]], j)
                    BASE[x, :, cuts[j]] = base
                    RATE[x, :, cuts[j]] = base * (0.2 + 0.8 * denv[x : x + 1, cuts[j]])

        def reciprocal(diagonal):
            guess = pl.reciprocal(diagonal, approx=True)
            return guess * (2.0 - diagonal * guess)

        with jax.named_scope("diagonal"):

            def diagonals(x, carry):
                for s in range(subs):
                    rows = pl.ds(s * SUB, SUB)
                    rate = RATE[x, rows, :]
                    total = None
                    for pair in range(half):
                        csum = jnp.concatenate([CF[pair, 5, rows, :]] * tiles, axis=1)
                        inverse = reciprocal(csum + rate)
                        R[pair, x + 1, rows, :] = inverse
                        total = inverse if pair == 0 else total + inverse
                    SUMR[x, rows, :] = total + total
                return carry

            lax.fori_loop(0, nx, diagonals, 0)

        with jax.named_scope("barrier"):
            most = jnp.logical_or(space == 1, space == n_space - 2)

            @pl.when(most)
            def _():
                pl.semaphore_wait(barrier, n_dir + 3)

            @pl.when(jnp.logical_not(most))
            def _():
                pl.semaphore_wait(barrier, n_dir + 2)

        with jax.named_scope("halo0"):
            start_far(lambda down: halo(0, down))

        start(lambda down: rows_copy(0, down))

        def sum_group(source, target, g, shift):
            def body(x, carry):
                total = source[g * group, x + shift]
                for d in range(1, group):
                    total = total + source[g * group + d, x + shift]
                if g:
                    total = total + target[x]
                target[x] = total
                return carry

            lax.fori_loop(0, nx, body, 0)

        def x_copy(n, k):
            ref = XE.at[block] if n == EARLY else XL.at[block] if n == LATE else XB.at[n, block]
            return pltpu.make_async_remote_copy(
                src_ref=ref,
                dst_ref=ref,
                send_sem=x_send.at[n, k - 1],
                recv_sem=x_recv.at[n, k - 1],
                device_id={"dir": lax.rem(block + k, n_dir)},
                device_id_type=MESH,
            )

        def z_copy(n, aside=False):
            ref = ZE.at[band] if n == EARLY else ZL.at[band] if n == LATE else ZB.at[n, band]
            return pltpu.make_async_remote_copy(
                src_ref=ref,
                dst_ref=ref,
                send_sem=z_send.at[n],
                recv_sem=z_recv.at[n],
                device_id={"dir": before if aside else block, "band": other_band},
                device_id_type=MESH,
            )

        def x_start(n):
            for k in sorted(range(1, n_dir), key=lambda k: -min(k, n_dir - k)):
                x_copy(n, k).start()

        def x_end(n):
            for k in range(1, n_dir):
                x_copy(n, k).wait_recv()
            terms = [
                XE[k] if n == EARLY else XL[k] if n == LATE else XB[n, k] for k in range(n_dir)
            ]
            total = terms[0]
            for term in terms[1:]:
                total = total + term
            return total

        def x_then_z(n):
            total = x_end(n)
            if n == EARLY:
                ZE[band] = total
                z_copy(n).start()
            elif n == LATE:
                ZL[band] = total
                z_copy(n).start()
            elif n >= SECOND:
                ZB[n, band] = total
                z_copy(n).start()
            else:
                ZB[n, band] = total

                @pl.when(shared)
                def _():
                    z_copy(n, True).start()

                @pl.when(jnp.logical_not(shared))
                def _():
                    z_copy(n).start()

        def exchange_end(n):
            z_copy(n).wait_recv()
            if n == EARLY:
                return ZE[0] + ZE[1]
            if n == LATE:
                return ZL[0] + ZL[1]
            return ZB[n, 0] + ZB[n, 1]

        def exchange_drain(n):
            for k in range(1, n_dir):
                x_copy(n, k).wait_send()
            z_copy(n).wait_send()

        def folded(value):
            return jnp.sum(value, axis=0, keepdims=True)

        with jax.named_scope("sum_a"):
            for g in range(ndir // group):
                loads_a[g].wait()
                sum_group(A, SUMA, g, 0 if g * group < half else 1)
            for x in range(nx):
                XB[0, block, x : x + 1, :] = folded(RATE[x] * SUMA[x])
            x_start(0)
            for x in range(nx):
                XB[THIRD, block, x : x + 1, :] = folded(BASE[x] * wide_weight * SUMR[x])
        with jax.named_scope("sum_p"):
            for g in range(ndir // group):
                loads_p[g].wait()
                sum_group(PV, SUMP, g, 0)
            for x in range(nx):
                share = folded(wide_weight * SUMP[x])
                XB[1, block, x : x + 1, :] = share
                TL[x : x + 1, :] = share * mean_scale[:, :1]
                TB[x] = jnp.broadcast_to(TL[x : x + 1, :], (SUB, plane))
            x_start(1)

        for x in range(nx):
            for buffer in (SUMA, SUMP, SUMG):
                buffer[x] = jnp.zeros((nbands, plane), jnp.float32)

        lane8 = lax.broadcasted_iota(jnp.int32, (SUB, LANES), 1)
        low_lanes = lane8 < LANES // 2
        edge_first = lane8 == 0
        edge_last = lane8 == LANES - 1

        def stream(forward_y, up_z, pair, rows, field, near_x):
            cx = CF[pair, 0, rows, :]
            cy = [CF[pair, 1 + i, rows, :] for i in range(3)]
            cz = CF[pair, 4, rows, :]
            turn = [pltpu.roll(v, LANES - 1 if forward_y else 1, 1) for v in field]
            halfway = [pltpu.roll(v, LANES // 2, 1) for v in field]
            values = []
            for j in range(tiles):
                moved = turn[j]
                if forward_y:
                    coef = cy[(0, 1, 2)[j % 3]]
                    if j % 3 != 2:
                        moved = jnp.where(edge_last, turn[j + 1], moved)
                else:
                    coef = cy[(2, 1, 0)[j % 3]]
                    if j % 3 != 0:
                        moved = jnp.where(edge_first, turn[j - 1], moved)
                value = cx * near_x[j] + coef * moved
                if up_z:
                    if j + 2 < tiles:
                        value = value + cz * jnp.where(low_lanes, halfway[j + 1], halfway[j + 2])
                    elif j + 1 < tiles:
                        value = value + cz * jnp.where(low_lanes, halfway[j + 1], 0.0)
                else:
                    if j >= 2:
                        value = value + cz * jnp.where(low_lanes, halfway[j - 2], halfway[j - 1])
                    elif j >= 1:
                        value = value + cz * jnp.where(low_lanes, 0.0, halfway[j - 1])
                values.append(value)
            return values

        def split(ref_rows):
            return [ref_rows[:, c] for c in cuts]

        def join(parts):
            return jnp.concatenate(parts, axis=1)

        def slab_a(forward_y, side, x):
            for s in range(subs):
                rows = pl.ds(s * SUB, SUB)
                total = None
                for pair in range(half):
                    d = pair + side * half
                    own, other = x + side, x + 1 - side
                    near = stream(
                        forward_y, pair % 2 == 0, pair, rows, split(A[d, own, rows, :]), split(A[d, other, rows, :])
                    )
                    value = join(near) * R[pair, x + 1, rows, :]
                    D[d, own, rows, :] = value
                    total = value if pair == 0 else total + value
                SUMA[x, rows, :] = SUMA[x, rows, :] + total

        def slab_b(forward_y, side, x):
            warm = split(TB[x])
            for s in range(subs):
                rows = pl.ds(s * SUB, SUB)
                source = split(WS[x + 2 - 2 * side, rows, :])
                own_source = split(WS[x + 1, rows, :])
                total_g, total_e, total_h = None, None, None
                for pair in range(half):
                    d = pair + side * half
                    own, other = x + side, x + 1 - side
                    beside_a = split(D[d, other, rows, :])
                    beside_r = split(R[pair, x + 2 - 2 * side, rows, :])
                    near_x = [beside_a[j] + source[j] * beside_r[j] for j in range(tiles)]
                    own_a = split(D[d, own, rows, :])
                    inverse = split(R[pair, x + 1, rows, :])
                    field = [own_a[j] + own_source[j] * inverse[j] for j in range(tiles)]
                    near = stream(forward_y, pair % 2 == 0, pair, rows, field, near_x)
                    value = [near[j] * inverse[j] for j in range(tiles)]
                    out[d, x, rows, :] = join(value)
                    excess = split(PV[d, x, rows, :])
                    excess = [excess[j] - warm[j] for j in range(tiles)]
                    both_duals = [field[j] + value[j] for j in range(tiles)]
                    part_g = [both_duals[j] * excess[j] for j in range(tiles)]
                    part_e = [inverse[j] * excess[j] for j in range(tiles)]
                    total_g = part_g if pair == 0 else [total_g[j] + part_g[j] for j in range(tiles)]
                    total_e = part_e if pair == 0 else [total_e[j] + part_e[j] for j in range(tiles)]
                    total_h = both_duals if pair == 0 else [total_h[j] + both_duals[j] for j in range(tiles)]
                SUMG[x, rows, :] = SUMG[x, rows, :] + join(total_g)
                SUMP[x, rows, :] = SUMP[x, rows, :] + join(total_e)
                SUMA[x, rows, :] = SUMA[x, rows, :] + join(total_h)

        def sweep(step, forward_y, hooks):
            def layer(i, carry):
                for side in range(2):
                    pl.when(i == last)(hooks["halo"][side])
                    x = i if side == 0 else last - i
                    (slab_b if step else slab_a)(forward_y, side, x)
                for at, hook in hooks["after"]:
                    pl.when(i == at)(hook)
                return carry

            lax.fori_loop(0, nx, layer, 0)

        def both(step, hooks):
            @pl.when(ahead)
            def _():
                sweep(step, True, hooks)

            @pl.when(jnp.logical_not(ahead))
            def _():
                sweep(step, False, hooks)

        def set_source(x, slot, row):
            WS[slot] = wide_weight * row

        def wait_halo0(side):
            def hook():
                @pl.when(has_low if side else has_high)
                def _():
                    halo(0, side == 0).wait_recv()

            return hook

        def send_halo1():
            start_far(lambda down: halo(1, down))

        def send_near0():
            start_near(lambda down: halo(0, down))

        def middle0():
            with jax.named_scope("middle0"):
                x_then_z(0)
                x_start(THIRD)

        def middle_t():
            with jax.named_scope("middleT"):
                x_then_z(1)

        with jax.named_scope("sweepA"):
            both(0, {"halo": [wait_halo0(0), wait_halo0(1)], "after": ((1, send_near0), (0, send_halo1), (MIDDLE0, middle0))})
        with jax.named_scope("fold1"):
            for x in range(nx):
                XB[SECOND, block, x : x + 1, :] = folded(BASE[x] * SUMA[x])
                SUMA[x] = jnp.zeros((nbands, plane), jnp.float32)
            x_start(SECOND)

        with jax.named_scope("halodiag"):
            arrive(lambda down: rows_copy(0, down))

            def halo_diagonal(way):
                own = nx + 1 if way == 0 else 0
                for j in range(tiles):
                    base = base_of(HR[way, 1, :, cuts[j]], j)
                    rate = base * (0.2 + 0.8 * HR[way, 0, :, cuts[j]])
                    for pair in range(half):
                        R[pair, own, :, cuts[j]] = reciprocal(CF[pair, 5] + rate)

            @pl.when(has_high)
            def _():
                halo_diagonal(0)

            @pl.when(has_low)
            def _():
                halo_diagonal(1)

        middle_t()
        with jax.named_scope("end0"):
            coupling = exchange_end(0)
        start_near(lambda down: halo(1, down))
        with jax.named_scope("source0"):
            cell_source = NDIR * NB * owv[...]
            first_source = coupling + cell_source
            for x in range(nx):
                SV[x] = first_source[x : x + 1]
            start(lambda down: rows_copy(1, down))
        with jax.named_scope("source1"):
            for x in range(nx):
                source = wide_weight * first_source[x : x + 1]
                WS[x + 1] = source

        def wait_halo1(side):
            layer, row = (0, 1) if side else (nx + 1, 0)

            def hook():
                with jax.named_scope("waithalo1"):
                    @pl.when(has_low if side else has_high)
                    def _():
                        halo(1, side == 0).wait_recv()
                        rows_copy(1, side == 0).wait_recv()
                        WS[layer] = wide_weight * SH[row]

                    @pl.when(jnp.logical_not(has_low if side else has_high))
                    def _():
                        WS[layer] = jnp.zeros((nbands, plane), jnp.float32)

            return hook

        def middle1():
            with jax.named_scope("middle1"):
                x_then_z(SECOND)
                x_then_z(THIRD)

        def gradient_sums(x):
            base = 0.8 * BASE[x]
            shift = SH_T[x : x + 1, :]
            slope = folded(base * (SUMG[x] - shift * SUMA[x]))
            return slope, folded(base * wide_weight * (SUMP[x] - shift * SUMR[x]))

        def send_early():
            with jax.named_scope("early"):
                SH_T[...] = exchange_end(1) - TL[...]
                for row in range(nx - 2):
                    slope, share = gradient_sums(row + 1)
                    XE[block, row : row + 1, :] = slope
                    XE[block, nx - 2 + row : nx - 1 + row, :] = share
                x_start(EARLY)

        with jax.named_scope("sweepB"):
            both(1, {"halo": [wait_halo1(0), wait_halo1(1)], "after": ((last - 1, middle1), (last - 1, send_early))})
        with jax.named_scope("late"):
            for row, x in ((0, 0), (1, last)):
                slope, share = gradient_sums(x)
                XL[block, row : row + 1, :] = slope
                XL[block, 2 + row : 3 + row, :] = share
            x_start(LATE)
        with jax.named_scope("early_x"):
            x_then_z(EARLY)
        with jax.named_scope("late_x"):
            x_then_z(LATE)
        with jax.named_scope("end1"):
            first_source = SV[:, 0]
            total = exchange_end(SECOND) + first_source * exchange_end(THIRD)
            scale = 0.2 + 0.8 * denv[...]
            second_source = scale * total + NDIR * NB * owv[...]
            for x in range(nx):
                WS[x + 1] = wide_weight * second_source[x : x + 1]
        with jax.named_scope("final"):

            def finish(x, carry):
                source = WS[x + 1]
                for d in range(ndir):
                    out[d, x] = out[d, x] + source * R[d % half, x + 1]
                return carry

            lax.fori_loop(0, nx, finish, 0)
        with jax.named_scope("last_z"):
            inner, outer = exchange_end(EARLY), exchange_end(LATE)
            slope = jnp.concatenate([outer[0:1], inner[: nx - 2], outer[1:2]], axis=0)
            share = jnp.concatenate([outer[2:3], inner[nx - 2 :], outer[3:4]], axis=0)
            grad[...] = (slope + second_source * share) * (-0.125 / ITERS)
        with jax.named_scope("drain"):
            for n in range(6):
                exchange_drain(n)
            for step in range(2):
                drain(lambda down: halo(step, down))
                drain(lambda down: rows_copy(step, down))

    return kernel


def write_out(dual, grad, dual_out, grad_out, sem):
    count = dual.shape[0]
    copies = [pltpu.make_async_copy(grad, grad_out, sem.at[count])]
    for d in range(count):
        copies.append(pltpu.make_async_copy(dual.at[d], dual_out.at[d], sem.at[d]))
    for copy in copies:
        copy.start()
    for copy in copies:
        copy.wait()


def solution(mesh):
    n_space, n_dir, n_band = mesh.shape["space"], mesh.shape["dir"], mesh.shape["band"]
    placed = (
        P("dir", "band", "space", None),
        P("dir", "band", "space", None),
        P("space", None),
        P("space", None),
        P(None, "band"),
        P("band"),
        P(),
        P("space", None),
    )

    def on_device(adj, pri, den, mat, rt, gs, hc, ow):
        ndir, nbands, nx, plane = adj.shape
        half = ndir // 2
        f32 = jnp.float32
        vmem = lambda *shape: pltpu.VMEM(shape, f32)
        dma = pltpu.SemaphoreType.DMA
        call = pl.pallas_call(
            make_kernel(ndir, nbands, nx, plane, n_space, n_dir, n_band),
            out_shape=(
                jax.ShapeDtypeStruct((ndir, nx, nbands, plane), f32),
                jax.ShapeDtypeStruct((nx, plane), f32),
            ),
            in_specs=[pl.BlockSpec(memory_space=pltpu.HBM)] * 8,
            out_specs=(pl.BlockSpec(memory_space=pltpu.VMEM),) * 2,
            scratch_shapes=[
                vmem(ndir, nx + 1, nbands, plane),
                vmem(ndir, nx, nbands, plane),
                vmem(ndir, nx + 1, nbands, plane),
                vmem(half, nx + 2, nbands, plane),
                vmem(nx, nbands, plane),
                vmem(nx, nbands, plane),
                vmem(nx + 2, nbands, plane),
                vmem(half, 6, nbands, LANES),
                vmem(nx, nbands, plane),
                vmem(nx, nbands, plane),
                vmem(nx, nbands, plane),
                vmem(nx, nbands, plane),
                vmem(nx, SUB, plane),
                vmem(nx, 1, plane),
                vmem(2, 1, plane),
                vmem(2, 2, 1, plane),
                vmem(2, 2, 1, plane),
                vmem(nx, plane),
                pltpu.VMEM((nx, plane), jnp.int32),
                vmem(*rt.shape),
                vmem(1, nbands),
                vmem(1, NB),
                vmem(nx, plane),
                vmem(nx, plane),
                vmem(nx, plane),
                vmem(4, n_dir, nx, plane),
                vmem(4, n_band, nx, plane),
                vmem(n_dir, 2 * (nx - 2), plane),
                vmem(n_dir, 4, plane),
                vmem(n_band, 2 * (nx - 2), plane),
                vmem(n_band, 4, plane),
                dma((2, 4)),
                dma((6,)),
                dma((2, 2)),
                dma((2, 2)),
                dma((2, 2)),
                dma((2, 2)),
                dma((6, n_dir - 1)),
                dma((6, n_dir - 1)),
                dma((6,)),
                dma((6,)),
            ],
            compiler_params=pltpu.CompilerParams(
                collective_id=0, has_side_effects=True, vmem_limit_bytes=40 * 1024 * 1024
            ),
        )
        turn = lambda v: jnp.transpose(v, (0, 2, 1, 3))
        operands = (
            turn(adj), turn(pri), den, mat, rt, gs.reshape(1, nbands), hc.reshape(1, NB), ow
        )
        dual, grad = call(*[pltpu.with_memory_space_constraint(v, pltpu.HBM) for v in operands])
        dual, grad = pl.pallas_call(
            write_out,
            out_shape=(
                jax.ShapeDtypeStruct(dual.shape, f32),
                jax.ShapeDtypeStruct(grad.shape, f32),
            ),
            in_specs=[pl.BlockSpec(memory_space=pltpu.VMEM)] * 2,
            out_specs=(pl.BlockSpec(memory_space=pltpu.HBM),) * 2,
            scratch_shapes=[dma((ndir + 1,))],
            compiler_params=pltpu.CompilerParams(vmem_limit_bytes=1024 * 1024),
        )(dual, grad)
        return turn(dual), grad

    return jax.shard_map(
        on_device,
        mesh=mesh,
        in_specs=placed,
        out_specs=(P("dir", "band", "space", None), P("space", None)),
        check_vma=False,
    )
```
